512 devices in a mesh: state: 16 (over y_lo, x), space: 32 (over z, y_hi, core).
Axes of the slice: x: 4, y: 8 (y_hi: 2, y_lo: 4; y = y_hi * 4 + y_lo), z: 8, core: 2. Of those that a mesh axis runs over, the one named last changes fastest.
Arguments:
- states_in: bfloat16 [1536, 32768], P('state', 'space'), may hold values from -12 to 12
- cell_matrices: bfloat16 [64, 512, 512], P('space'), may hold values from -0.5 to 1.5, as said below
- connectivity: int32 [64, 512], P('space'), may hold values from 0 to 32767, as said below
- potential: float32 [32768], P('space'), may hold values from 0.2 to 1.2
Outputs:
- filtered: bfloat16 [1536, 32768], P('state', 'space')
- intersection: float32 [1536, 1536], P('state', 'space')
- projected: float32 [1536, 1536], P('state', 'space')
The draws below stay inside these ranges and needn't reach their ends.
Inputs may be any that keep to these rules, and one draw needn't show every extreme that they name: `cell_matrices`: each cell's matrix is symmetric. `connectivity`: the cells of rows s * 2 to (s + 1) * 2 - 1 name only nodes from s * 1024 - 128 to (s + 1) * 1024 + 127. A node may be named by several cells, or twice in one cell, or by none.
All inputs are finite; a program needn't handle non-finite values.
Results may differ from the reference program's by a relative error of at most 0.019.
Values may be sent and summed in bfloat16 or wider, within the bound.
A program may use at most 64 MiB of HBM per device.

```python
import jax
import jax.numpy as jnp
from jax import lax

CELL_NODES = 512
CELLS_DEV = 2
DEGREE = 4
NSTATES = 1536
NODE_DEV = 1024
NODES = 32768
CELLS = 64
RIM = 128


def draw_states_in(key, part):
    mode_count = NSTATES // 2
    first_key = jax.random.fold_in(key, 11)
    second_key = jax.random.fold_in(key, 12)
    third_key = jax.random.fold_in(key, 13)
    base = jax.random.normal(first_key, (NSTATES, NODES), jnp.float32)
    mixing = jax.random.normal(third_key, (NSTATES, mode_count), jnp.float32)
    shared_modes = jax.random.normal(second_key, (mode_count, NODES), jnp.float32)
    shared = jnp.dot(mixing, shared_modes) * (1.5 / mode_count ** 0.5)
    ramp = jnp.sqrt(1.0 + 2.0 * jnp.arange(NODES, dtype=jnp.float32) / NODES)
    values = (base + shared) * ramp[None, :]
    return jnp.clip(values, -12.0, 12.0).astype(jnp.bfloat16)


def draw_cell_matrices(key, part):
    first_key = jax.random.fold_in(key, 21)
    second_key = jax.random.fold_in(key, 22)
    spread = 0.35 / CELL_NODES ** 0.5
    random_part = jnp.clip(jax.random.normal(first_key, (CELLS, CELL_NODES, CELL_NODES), jnp.float32), -4.0, 4.0) * spread
    diagonal = jax.random.uniform(second_key, (CELLS, 1, CELL_NODES), jnp.float32, 0.3, 1.0)
    identity = jnp.eye(CELL_NODES, dtype=jnp.float32)[None, :, :]
    return (random_part + jnp.swapaxes(random_part, 1, 2) + identity * diagonal).astype(jnp.bfloat16)


def draw_connectivity(key, part):
    shard = jnp.arange(CELLS, dtype=jnp.int32) // CELLS_DEV
    lower = jnp.maximum(shard * NODE_DEV - RIM, 0)
    upper = jnp.minimum((shard + 1) * NODE_DEV + RIM, NODES)
    return jax.random.randint(jax.random.fold_in(key, 31), (CELLS, CELL_NODES), lower[:, None], upper[:, None], jnp.int32)


def steps_of(own_key, shape, split, low, top_value):
    factor_of, own = 1.0, jax.random.fold_in(own_key, 6)
    for dim, blocks in split:
        steps = jnp.exp(jax.random.uniform(jax.random.fold_in(own, dim), (blocks,), jnp.float32, low / len(split), top_value / len(split)))
        factor_of = factor_of * jnp.repeat(steps, shape[dim] // blocks).reshape([-1 if axis == dim else 1 for axis in range(len(shape))])
    return factor_of


def setup_inputs(seed: int = 0) -> dict:
    key_of = jax.random.split(jax.random.key(seed), 5)
    return {
        "states_in": draw_states_in(jax.random.fold_in(key_of[4], 71), 0),
        "cell_matrices": draw_cell_matrices(jax.random.fold_in(key_of[4], 71), 0),
        "connectivity": draw_connectivity(jax.random.fold_in(key_of[4], 71), 0),
        "potential": jnp.clip(0.2 + 1 * jax.random.uniform(key_of[3], (NODES,), jnp.float32) ** steps_of(key_of[3], (NODES,), ((0, 32),), -0.2, 0.2), 0.2, 1.2),
    }


spectrum_center = 3.0
spectrum_half = 3.5


def apply_hamiltonian(states, cell_matrices, connectivity, potential):
    picked = states[:, connectivity].astype(jnp.float32)
    products = jnp.einsum("scp,cpq->scq", picked, cell_matrices.astype(jnp.float32), precision=lax.Precision.HIGHEST)
    summed = jnp.zeros(states.shape, jnp.float32)
    summed = summed.at[:, connectivity.reshape(-1)].add(products.reshape(states.shape[0], -1))
    return summed + potential[None, :] * states.astype(jnp.float32)


def reference(states_in, cell_matrices, connectivity, potential):
    earlier = states_in
    first = (apply_hamiltonian(earlier, cell_matrices, connectivity, potential) - spectrum_center * earlier.astype(jnp.float32)) / spectrum_half
    current = first.astype(jnp.bfloat16)
    for section_index in range(DEGREE - 1):
        image = apply_hamiltonian(current, cell_matrices, connectivity, potential)
        following = 2.0 * (image - spectrum_center * current.astype(jnp.float32)) / spectrum_half - earlier.astype(jnp.float32)
        earlier = current
        current = following.astype(jnp.bfloat16)
    filtered = current
    energy = apply_hamiltonian(filtered, cell_matrices, connectivity, potential)
    intersection = jnp.dot(filtered, filtered.T, preferred_element_type=jnp.float32) / NODES
    projected = jnp.dot(energy, filtered.astype(jnp.float32).T, precision=lax.Precision.HIGHEST) / NODES
    return filtered, intersection, projected
```

```python
import functools

import jax
import jax.numpy as jnp
from jax import lax
from jax.experimental import pallas as pl
from jax.experimental.pallas import tpu as pltpu
from jax.sharding import Mesh
from jax.sharding import PartitionSpec as P

DEGREE = 4
STATE = ("state_0", "state_1")
CENTER = 3.0
HALF = 3.5
F32 = jnp.float32
BF16 = jnp.bfloat16
MESH_ID = pl.DeviceIdType.MESH


def joined_along(pieces, dim):
    shape = list(pieces.shape[1:])
    shape[dim] *= pieces.shape[0]
    return jnp.moveaxis(pieces, 0, dim).reshape(shape)


def gather_in_order(shard, axes, turns):
    pieces = shard[None]
    for k in turns:
        pieces = lax.all_gather(pieces, axes[k], axis=0, tiled=True)
    carried = [lax.axis_size(axes[k]) for k in reversed(turns)]
    pieces = pieces.reshape(*carried, *shard.shape)
    turned = sorted(range(len(turns)), key=lambda place: turns[len(turns) - 1 - place])
    return pieces.transpose(*turned, *range(len(turns), pieces.ndim)).reshape(-1, *shard.shape)


def gathered_by_axis(shard, axes, turns, dim):
    return joined_along(gather_in_order(shard, axes, turns), dim)


def split_up(shard, dim, length):
    shape = shard.shape
    pieces = shard.reshape(*shape[:dim], length, shape[dim] // length, *shape[dim + 1 :])
    return jnp.moveaxis(pieces, dim, 0)


def summed_on_arrival(shard, axis, dim):
    length = lax.axis_size(axis)
    pieces = lax.all_to_all(split_up(shard, dim, length), axis, 0, 0, tiled=True)
    return jnp.sum(pieces.astype(jnp.float32), axis=0)


def in_one_piece(arrays, axis, dim, along):
    both = jnp.concatenate(arrays, axis=along)
    filled, at, done = (summed_on_arrival(both, axis, dim), 0, [])
    for a in arrays:
        done.append(lax.slice_in_dim(filled, at, at + a.shape[along], axis=along))
        at += a.shape[along]
    return tuple(done)


def filter_kernel(
    states_ref, cells_ref, conn_ref, pot_ref,
    filt_ref, energy_ref,
    pick_ref, put_ref, v_ref, acc_ref, part_ref, snd_ref, rcv_ref, esnd_ref, ercv_ref, ssem, rsem,
):
    rows, nodes = states_ref.shape
    cells, local = conn_ref.shape
    ext = pick_ref.shape[0]
    rim = (ext - nodes) // 2
    zone = 2 * rim
    inner = slice(zone, ext - zone)
    zones = (slice(0, zone), slice(ext - zone, ext))
    ring = lax.axis_size("space")
    me = lax.axis_index("space")
    left, right = lax.rem(me + ring - 1, ring), lax.rem(me + 1, ring)
    to = (left, right)

    barrier = pltpu.get_barrier_semaphore()
    for near in to:
        pl.semaphore_signal(barrier, inc=1, device_id={"space": near}, device_id_type=MESH_ID)

    offset = me * nodes - rim
    v_ref[0, :, rim : rim + nodes] = states_ref[...]

    tile = 128
    for c in range(cells):
        named = conn_ref[c : c + 1, :] - offset

        @pl.loop(0, ext // tile)
        def _(r):
            start = pl.multiple_of(r * tile, tile)
            node = lax.broadcasted_iota(jnp.int32, (tile, local), 0) + start
            pick_ref[pl.ds(start, tile), c * local : (c + 1) * local] = jnp.where(
                node == named, 1.0, 0.0
            ).astype(BF16)

    pl.semaphore_wait(barrier, 2)

    def copy(step, side, src, dst):
        return pltpu.make_async_remote_copy(
            src_ref=src, dst_ref=dst, send_sem=ssem.at[step, side], recv_sem=rsem.at[step, 1 - side],
            device_id={"space": to[side]}, device_id_type=MESH_ID,
        )

    flights = [[] for _ in range(DEGREE + 2)]
    flights[0] = [
        copy(0, 0, states_ref.at[:, pl.ds(0, rim)], v_ref.at[0, :, pl.ds(ext - rim, rim)]),
        copy(0, 1, states_ref.at[:, pl.ds(nodes - rim, rim)], v_ref.at[0, :, pl.ds(0, rim)]),
    ]
    for f in flights[0]:
        f.start()

    for c in range(cells):
        named = jnp.transpose(jnp.broadcast_to(conn_ref[c : c + 1, :] - offset, (tile, local)))

        @pl.loop(0, ext // tile)
        def _(n):
            start = pl.multiple_of(n * tile, tile)
            node = lax.broadcasted_iota(jnp.int32, (local, tile), 1) + start
            put_ref[c * local : (c + 1) * local, pl.ds(start, tile)] = jnp.where(
                node == named, 1.0, 0.0
            ).astype(BF16)

    still = jnp.zeros((1, rim), F32)
    pot = jnp.concatenate([still, pot_ref[...], still], axis=1)

    def level(k, image, where):
        held = v_ref[k - 1, :, where].astype(F32)
        if k == 1:
            made = (image - CENTER * held) * (1.0 / HALF)
        else:
            made = (image - CENTER * held) * (2.0 / HALF) - v_ref[k - 2, :, where].astype(F32)
        v_ref[k, :, where] = made.astype(BF16)

    def product(picked):
        return jnp.concatenate(
            [
                jnp.dot(picked[:, c * local : (c + 1) * local], cells_ref[c], preferred_element_type=F32)
                for c in range(cells)
            ],
            axis=1,
        )

    def picked(k, where):
        return jnp.dot(v_ref[k, :, where], pick_ref[where, :], preferred_element_type=F32)

    for k in range(DEGREE + 1):
        acc_ref[...] = product(picked(k, inner).astype(BF16))
        for f in flights[k]:
            f.wait_recv()
        if k:
            for side in (0, 1):
                level(k, part_ref[side] + rcv_ref[k - 1, side].astype(F32), zones[side])
        late = (picked(k, zones[0]) + picked(k, zones[1])).astype(BF16)
        products = (acc_ref[...] + product(late)).astype(BF16)

        def image(where):
            placed = jnp.dot(products, put_ref[:, where], preferred_element_type=F32)
            return placed + pot[:, where] * v_ref[k, :, where].astype(F32)

        for side in (0, 1):
            mine = image(zones[side])
            part_ref[side] = mine
            if k < DEGREE:
                snd_ref[k, side] = mine.astype(BF16)
                flights[k + 1].append(copy(k + 1, side, snd_ref.at[k, side], rcv_ref.at[k, 1 - side]))
            else:
                esnd_ref[side] = mine[:, side * rim : (side + 1) * rim].astype(BF16)
                flights[k + 1].append(copy(k + 1, side, esnd_ref.at[side], ercv_ref.at[1 - side]))
            flights[k + 1][-1].start()
        if k < DEGREE:
            level(k + 1, image(inner), inner)
        else:
            filt_ref[...] = v_ref[k, :, rim : rim + nodes]
            energy_ref[:, rim : nodes - rim] = image(inner).astype(BF16)

    for f in flights[DEGREE + 1]:
        f.wait_recv()
    for side in (0, 1):
        at = slice(0, rim) if side == 0 else slice(nodes - rim, nodes)
        own = slice(rim, zone) if side == 0 else slice(0, rim)
        energy_ref[:, at] = (part_ref[side, :, own] + ercv_ref[side].astype(F32)).astype(BF16)
    for step in flights:
        for f in step:
            f.wait_send()


def filtered_states(states, cell_matrices, connectivity, potential):
    rows, nodes = states.shape
    cells, local, _ = cell_matrices.shape
    rim = local // 4
    ext = nodes + 2 * rim
    vmem = pl.BlockSpec(memory_space=pltpu.VMEM)
    return pl.pallas_call(
        filter_kernel,
        out_shape=(
            jax.ShapeDtypeStruct((rows, nodes), BF16),
            jax.ShapeDtypeStruct((rows, nodes), BF16),
        ),
        in_specs=[vmem] * 4,
        out_specs=(vmem, vmem),
        scratch_shapes=[
            pltpu.VMEM((ext, cells * local), BF16),
            pltpu.VMEM((cells * local, ext), BF16),
            pltpu.VMEM((DEGREE + 1, rows, ext), BF16),
            pltpu.VMEM((rows, cells * local), F32),
            pltpu.VMEM((2, rows, 2 * rim), F32),
            pltpu.VMEM((DEGREE, 2, rows, 2 * rim), BF16),
            pltpu.VMEM((DEGREE, 2, rows, 2 * rim), BF16),
            pltpu.VMEM((2, rows, rim), BF16),
            pltpu.VMEM((2, rows, rim), BF16),
            pltpu.SemaphoreType.DMA((DEGREE + 2, 2)),
            pltpu.SemaphoreType.DMA((DEGREE + 2, 2)),
        ],
        compiler_params=pltpu.CompilerParams(collective_id=0, has_side_effects=True),
    )(states, cell_matrices, connectivity, potential.reshape(1, -1))


def per_device(states_in, cell_matrices, connectivity, potential):
    current, energy = filtered_states(states_in, cell_matrices, connectivity, potential)
    total_nodes = states_in.shape[1] * lax.axis_size("space")
    contract = (((1,), (1,)), ((), ()))
    gathered = gathered_by_axis(current, STATE, (0, 1), 0)
    intersection = lax.dot_general(current, gathered, contract, preferred_element_type=jnp.float32)
    projected = lax.dot_general(energy, gathered, contract, preferred_element_type=jnp.float32)
    intersection = intersection / total_nodes
    projected = projected / total_nodes
    intersection, projected = in_one_piece(
        (intersection.astype(jnp.bfloat16), projected.astype(jnp.bfloat16)), "space", 1, 0
    )
    return (current, intersection, projected)


def solution(mesh):
    states = mesh.shape["state"]
    wide = 4 if states % 4 == 0 else 1
    finer = Mesh(
        mesh.devices.reshape(states // wide, wide, mesh.shape["space"]), ("state_0", "state_1", "space")
    )
    placed = (P(STATE, "space"), P("space", None, None), P("space", None), P("space"))
    return jax.shard_map(
        per_device,
        mesh=finer,
        in_specs=placed,
        out_specs=(P(STATE, "space"), P(STATE, "space"), P(STATE, "space")),
        check_vma=False,
    )
```

```python
import jax
import jax.numpy as jnp
from jax import lax
from jax.experimental import pallas as pl
from jax.experimental.pallas import tpu as pltpu
from jax.sharding import Mesh
from jax.sharding import PartitionSpec as P

DEGREE = 4
WIDE = 4
STATE = ("state_0", "state_1")
CENTER = 3.0
HALF = 3.5
F32 = jnp.float32
BF16 = jnp.bfloat16
MESH_ID = pl.DeviceIdType.MESH
TRANSPOSED = (((1,), (1,)), ((), ()))


def kernel(
    states_ref, cells_ref, conn_ref, pot_ref,
    filt_ref, inter_ref, proj_ref,
    pick_ref, put_ref, v_ref, acc_ref, part_ref, snd_ref, rcv_ref, esnd_ref, ercv_ref,
    row_ref, col_ref, sum_ref, csnd_ref, crcv_ref, psnd_ref, prcv_ref,
    ssem, rsem, lsend, lrecv, wsend, wrecv, csend, crecv, psend, precv,
):
    rows, nodes = states_ref.shape
    cells, local = conn_ref.shape
    ext = pick_ref.shape[0]
    rim = (ext - nodes) // 2
    zone = 2 * rim
    inner = slice(zone, ext - zone)
    zones = (slice(0, zone), slice(ext - zone, ext))
    half = rows // 2
    ring, line, wide = lax.axis_size("space"), lax.axis_size("state_0"), lax.axis_size("state_1")
    chips = ring // 2
    me, a, b = lax.axis_index("space"), lax.axis_index("state_0"), lax.axis_index("state_1")
    chip, core = me // 2, lax.rem(me, 2)
    to = (lax.rem(me + ring - 1, ring), lax.rem(me + 1, ring))
    beside = (lax.rem(b + wide - 1, wide), lax.rem(b + 1, wide))
    opposite = lax.rem(b + 2, wide)
    sibling = me + 1 - 2 * core
    source = lax.rem(chip, wide)
    keeps = b == source

    barrier = pltpu.get_barrier_semaphore()

    def greet(**device):
        pl.semaphore_signal(barrier, inc=1, device_id=device, device_id_type=MESH_ID)

    for side in (0, 1):
        greet(space=to[side])
        greet(state_1=beside[side])

    @pl.when(a > 0)
    def _():
        greet(state_0=a - 1)

    @pl.when(a < line - 1)
    def _():
        greet(state_0=a + 1)

    for p in range(chips):

        @pl.when(jnp.logical_not(keeps & (chip == p)))
        def _():
            greet(state_1=source, space=2 * p + core)

    offset = me * nodes - rim
    v_ref[0, :, rim : rim + nodes] = states_ref[...]

    tile = rim
    for c in range(cells):
        named = conn_ref[c : c + 1, :] - offset

        @pl.loop(0, ext // tile)
        def _(r):
            start = pl.multiple_of(r * tile, tile)
            node = lax.broadcasted_iota(jnp.int32, (tile, local), 0) + start
            pick_ref[pl.ds(start, tile), c * local : (c + 1) * local] = jnp.where(
                node == named, 1.0, 0.0
            ).astype(BF16)

    greeted = jnp.int32(4 + chips) + (a > 0).astype(jnp.int32) + (a < line - 1).astype(jnp.int32)
    pl.semaphore_wait(barrier, greeted - keeps.astype(jnp.int32))

    def copy(step, side, src, dst):
        return pltpu.make_async_remote_copy(
            src_ref=src, dst_ref=dst, send_sem=ssem.at[step, side], recv_sem=rsem.at[step, 1 - side],
            device_id={"space": to[side]}, device_id_type=MESH_ID,
        )

    flights = [[] for _ in range(DEGREE + 2)]
    flights[0] = [
        copy(0, 0, states_ref.at[:, pl.ds(0, rim)], v_ref.at[0, :, pl.ds(ext - rim, rim)]),
        copy(0, 1, states_ref.at[:, pl.ds(nodes - rim, rim)], v_ref.at[0, :, pl.ds(0, rim)]),
    ]
    for f in flights[0]:
        f.start()

    for c in range(cells):
        named = jnp.transpose(jnp.broadcast_to(conn_ref[c : c + 1, :] - offset, (tile, local)))

        @pl.loop(0, ext // tile)
        def _(n):
            start = pl.multiple_of(n * tile, tile)
            node = lax.broadcasted_iota(jnp.int32, (local, tile), 1) + start
            put_ref[c * local : (c + 1) * local, pl.ds(start, tile)] = jnp.where(
                node == named, 1.0, 0.0
            ).astype(BF16)

    still = jnp.zeros((1, rim), F32)
    pot = jnp.concatenate([still, pot_ref[...], still], axis=1)

    def level(k, image, where):
        held = v_ref[k - 1, :, where].astype(F32)
        if k == 1:
            made = (image - CENTER * held) * (1.0 / HALF)
        else:
            made = (image - CENTER * held) * (2.0 / HALF) - v_ref[k - 2, :, where].astype(F32)
        v_ref[k, :, where] = made.astype(BF16)

    def product(picked):
        return jnp.concatenate(
            [
                jnp.dot(picked[:, c * local : (c + 1) * local], cells_ref[c], preferred_element_type=F32)
                for c in range(cells)
            ],
            axis=1,
        )

    def picked(k, where):
        return jnp.dot(v_ref[k, :, where], pick_ref[where, :], preferred_element_type=F32)

    parts = ((rim, nodes - zone), (0, rim), (nodes - rim, rim))

    def along(way, block, part):
        block = lax.rem(block + line, line)
        spot = col_ref.at[block, :, pl.ds(*parts[part])]
        return pltpu.make_async_remote_copy(
            src_ref=spot, dst_ref=spot, send_sem=lsend.at[way, block, part], recv_sem=lrecv.at[block, part],
            device_id={"state_0": lax.rem(a + line + 2 * way - 1, line)}, device_id_type=MESH_ID,
        )

    def goes(way, hop):
        return (a - hop >= 0) & (a + 1 < line) if way else (a + hop < line) & (a >= 1)

    def come(way, hop):
        return a - hop >= 0 if way else a + hop < line

    def pass_along(hop, part):
        for way in (0, 1):
            block = a - hop if way else a + hop
            if hop:

                @pl.when(come(way, hop))
                def _():
                    along(way, block, part).wait_recv()

            @pl.when(goes(way, hop))
            def _():
                along(way, block, part).start()

    def around(turn, kind, part):
        block = (b, b, beside[0], beside[1])[turn]
        first, count = ((0, rows), (0, rows), (0, half), (half, half))[turn]
        spot = row_ref.at[block, pl.ds(kind * rows + first, count), pl.ds(*parts[part])]
        return pltpu.make_async_remote_copy(
            src_ref=spot, dst_ref=spot, send_sem=wsend.at[turn, kind, part], recv_sem=wrecv.at[turn, kind, part],
            device_id={"state_1": beside[1 - turn % 2]}, device_id_type=MESH_ID,
        )

    def arrive(turn, kind, part):
        block = (beside[0], beside[1], opposite, opposite)[turn]
        first, count = ((0, rows), (0, rows), (0, half), (half, half))[turn]
        spot = row_ref.at[block, pl.ds(kind * rows + first, count), pl.ds(*parts[part])]
        pltpu.make_async_remote_copy(
            src_ref=spot, dst_ref=spot, send_sem=wsend.at[turn, kind, part], recv_sem=wrecv.at[turn, kind, part],
            device_id={"state_1": beside[1 - turn % 2]}, device_id_type=MESH_ID,
        ).wait_recv()

    def send_around(kind, part):
        for turn in (0, 1):
            around(turn, kind, part).start()

    def pass_around(kind, part):
        for turn in (0, 1):
            arrive(turn, kind, part)
            around(turn + 2, kind, part).start()

    def share(part):
        first, count = parts[part]
        own = v_ref[DEGREE, :, rim + first : rim + first + count]
        col_ref[a, :, first : first + count] = own
        row_ref[b, 0:rows, first : first + count] = own
        pass_along(0, part)
        send_around(0, part)

    for k in range(DEGREE + 1):
        acc_ref[...] = product(picked(k, inner).astype(BF16))
        for f in flights[k]:
            f.wait_recv()
        if k:
            for side in (0, 1):
                level(k, part_ref[side] + rcv_ref[k - 1, side].astype(F32), zones[side])
        if k == DEGREE:
            share(1)
            share(2)
        late = (picked(k, zones[0]) + picked(k, zones[1])).astype(BF16)
        products = (acc_ref[...] + product(late)).astype(BF16)

        def image(where):
            placed = jnp.dot(products, put_ref[:, where], preferred_element_type=F32)
            return placed + pot[:, where] * v_ref[k, :, where].astype(F32)

        for side in (0, 1):
            mine = image(zones[side])
            part_ref[side] = mine
            if k < DEGREE:
                snd_ref[k, side] = mine.astype(BF16)
                flights[k + 1].append(copy(k + 1, side, snd_ref.at[k, side], rcv_ref.at[k, 1 - side]))
            else:
                esnd_ref[side] = mine[:, side * rim : (side + 1) * rim].astype(BF16)
                flights[k + 1].append(copy(k + 1, side, esnd_ref.at[side], ercv_ref.at[1 - side]))
            flights[k + 1][-1].start()
        if k < DEGREE:
            level(k + 1, image(inner), inner)
        else:
            filt_ref[...] = v_ref[k, :, rim : rim + nodes]
            row_ref[b, rows : 2 * rows, rim : nodes - rim] = image(inner).astype(BF16)
            send_around(1, 0)
        if k == DEGREE - 1:
            share(0)

    pass_along(1, 0)
    pass_around(0, 0)
    for f in flights[DEGREE + 1]:
        f.wait_recv()
    for side in (0, 1):
        first = side * (nodes - rim)
        own = slice(rim, zone) if side == 0 else slice(0, rim)
        row_ref[b, rows : 2 * rows, first : first + rim] = (
            part_ref[side, :, own] + ercv_ref[side].astype(F32)
        ).astype(BF16)
        send_around(1, 1 + side)
    for part in (1, 2):
        pass_along(1, part)
        pass_around(0, part)
    for hop in range(2, max(line, 3)):
        for part in range(3):
            pass_along(hop, part)
            if hop == 2:
                pass_around(1, part)
    for kind in (0, 1):
        for part in range(3):
            for turn in (2, 3):
                arrive(turn, kind, part)

    def to_sibling(i):
        return pltpu.make_async_remote_copy(
            src_ref=csnd_ref.at[i], dst_ref=crcv_ref.at[i], send_sem=csend.at[i], recv_sem=crecv.at[i],
            device_id={"space": sibling}, device_id_type=MESH_ID,
        )

    for i in range(line):
        for j in range(wide):
            sum_ref[i, j] = lax.dot_general(col_ref[i], row_ref[j], TRANSPOSED, preferred_element_type=F32)
            csnd_ref[i, j] = sum_ref[i, j, pl.ds(pl.multiple_of((1 - core) * half, half), half), :].astype(BF16)
        to_sibling(i).start()

    def to_owner(i, j):
        return pltpu.make_async_remote_copy(
            src_ref=psnd_ref.at[i, j], dst_ref=prcv_ref.at[chip], send_sem=psend.at[i, j], recv_sem=precv.at[chip],
            device_id={"state_1": j, "space": 2 * (i * wide + b) + core}, device_id_type=MESH_ID,
        )

    def stays(i, j):
        return (b == j) & (chip == i * wide + b)

    for i in range(line):
        to_sibling(i).wait_recv()
        for j in range(wide):
            mine = sum_ref[i, j, pl.ds(pl.multiple_of(core * half, half), half), :]
            psnd_ref[i, j] = (mine + crcv_ref[i, j].astype(F32)).astype(BF16)

            @pl.when(stays(i, j))
            def _():
                prcv_ref[chip] = psnd_ref[i, j]

            @pl.when(jnp.logical_not(stays(i, j)))
            def _():
                to_owner(i, j).start()

    total = jnp.zeros((half, 2 * rows), F32)
    for p in range(chips):

        @pl.when(jnp.logical_not(keeps & (chip == p)))
        def _():
            pltpu.make_async_remote_copy(
                src_ref=prcv_ref.at[p], dst_ref=prcv_ref.at[p], send_sem=precv.at[p], recv_sem=precv.at[p],
                device_id={"space": sibling}, device_id_type=MESH_ID,
            ).wait_recv()

        total += prcv_ref[p].astype(F32)
    turned = jnp.transpose(total * (1.0 / (nodes * ring)))
    inter_ref[...] = turned[0:rows]
    proj_ref[...] = turned[rows : 2 * rows]

    for step in flights:
        for f in step:
            f.wait_send()
    for way in (0, 1):
        for hop in range(line - 1):
            for part in range(3):

                @pl.when(goes(way, hop))
                def _():
                    along(way, a - hop if way else a + hop, part).wait_send()

    for turn in range(4):
        for kind in (0, 1):
            for part in range(3):
                around(turn, kind, part).wait_send()
    for i in range(line):
        to_sibling(i).wait_send()
        for j in range(wide):

            @pl.when(jnp.logical_not(stays(i, j)))
            def _():
                to_owner(i, j).wait_send()


def per_device(states, cell_matrices, connectivity, potential):
    rows, nodes = states.shape
    cells, local, _ = cell_matrices.shape
    line, wide, ring = (lax.axis_size(name) for name in (*STATE, "space"))
    chips, half = ring // 2, rows // 2
    rim = local // 4
    ext = nodes + 2 * rim
    vmem = pl.BlockSpec(memory_space=pltpu.VMEM)
    dma = pltpu.SemaphoreType.DMA
    return pl.pallas_call(
        kernel,
        out_shape=(
            jax.ShapeDtypeStruct((rows, nodes), BF16),
            jax.ShapeDtypeStruct((rows, half), F32),
            jax.ShapeDtypeStruct((rows, half), F32),
        ),
        in_specs=[vmem] * 4,
        out_specs=(vmem, vmem, vmem),
        scratch_shapes=[
            pltpu.VMEM((ext, cells * local), BF16),
            pltpu.VMEM((cells * local, ext), BF16),
            pltpu.VMEM((DEGREE + 1, rows, ext), BF16),
            pltpu.VMEM((rows, cells * local), F32),
            pltpu.VMEM((2, rows, 2 * rim), F32),
            pltpu.VMEM((DEGREE, 2, rows, 2 * rim), BF16),
            pltpu.VMEM((DEGREE, 2, rows, 2 * rim), BF16),
            pltpu.VMEM((2, rows, rim), BF16),
            pltpu.VMEM((2, rows, rim), BF16),
            pltpu.VMEM((wide, 2 * rows, nodes), BF16),
            pltpu.VMEM((line, rows, nodes), BF16),
            pltpu.VMEM((line, wide, rows, 2 * rows), F32),
            pltpu.VMEM((line, wide, half, 2 * rows), BF16),
            pltpu.VMEM((line, wide, half, 2 * rows), BF16),
            pltpu.VMEM((line, wide, half, 2 * rows), BF16),
            pltpu.VMEM((chips, half, 2 * rows), BF16),
            dma((DEGREE + 2, 2)), dma((DEGREE + 2, 2)),
            dma((2, line, 3)), dma((line, 3)),
            dma((4, 2, 3)), dma((4, 2, 3)),
            dma((line,)), dma((line,)),
            dma((line, wide)), dma((chips,)),
        ],
        compiler_params=pltpu.CompilerParams(collective_id=0, has_side_effects=True),
    )(states, cell_matrices, connectivity, potential.reshape(1, -1))


def solution(mesh):
    line = mesh.shape["state"] // WIDE
    finer = Mesh(mesh.devices.reshape(line, WIDE, mesh.shape["space"]), (*STATE, "space"))
    placed = (P(STATE, "space"), P("space", None, None), P("space", None), P("space"))
    return jax.shard_map(
        per_device,
        mesh=finer,
        in_specs=placed,
        out_specs=(P(STATE, "space"), P(STATE, "space"), P(STATE, "space")),
        check_vma=False,
    )
```

```python
import jax
import jax.numpy as jnp
from jax import lax
from jax.experimental import pallas as pl
from jax.experimental.pallas import tpu as pltpu
from jax.sharding import Mesh
from jax.sharding import PartitionSpec as P

DEGREE = 4
WIDE = 4
STATE = ("state_0", "state_1")
CENTER = 3.0
HALF = 3.5
F32 = jnp.float32
BF16 = jnp.bfloat16
MESH_ID = pl.DeviceIdType.MESH
TRANSPOSED = (((1,), (1,)), ((), ()))


def kernel(
    states_ref, cells_ref, conn_ref, pot_ref,
    filt_ref, inter_ref, proj_ref,
    pick_ref, put_ref, v_ref, acc_ref, part_ref, snd_ref, rcv_ref, esnd_ref, ercv_ref,
    row_ref, col_ref, sum_ref, csnd_ref, crcv_ref, psnd_ref, prcv_ref,
    ssem, rsem, lsend, lrecv, wsend, wrecv, csend, crecv, psend, precv,
):
    rows, nodes = states_ref.shape
    cells, local = conn_ref.shape
    ext = pick_ref.shape[0]
    rim = (ext - nodes) // 2
    zone = 2 * rim
    inner = slice(zone, ext - zone)
    zones = (slice(0, zone), slice(ext - zone, ext))
    half = rows // 2
    ring, line, wide = lax.axis_size("space"), lax.axis_size("state_0"), lax.axis_size("state_1")
    chips = ring // 2
    me, a, b = lax.axis_index("space"), lax.axis_index("state_0"), lax.axis_index("state_1")
    chip, core = me // 2, lax.rem(me, 2)
    to = (lax.rem(me + ring - 1, ring), lax.rem(me + 1, ring))
    beside = (lax.rem(b + wide - 1, wide), lax.rem(b + 1, wide))
    opposite = lax.rem(b + 2, wide)
    sibling = me + 1 - 2 * core
    source = lax.rem(chip, wide)
    keeps = b == source

    barrier = pltpu.get_barrier_semaphore()

    def greet(**device):
        pl.semaphore_signal(barrier, inc=1, device_id=device, device_id_type=MESH_ID)

    for side in (0, 1):
        greet(space=to[side])
        greet(state_1=beside[side])

    @pl.when(a > 0)
    def _():
        greet(state_0=a - 1)

    @pl.when(a < line - 1)
    def _():
        greet(state_0=a + 1)

    for p in range(chips):

        @pl.when(jnp.logical_not(keeps & (chip == p)))
        def _():
            greet(state_1=source, space=2 * p + core)

    offset = me * nodes - rim
    v_ref[0, :, rim : rim + nodes] = states_ref[...]

    tile = rim
    for c in range(cells):
        named = conn_ref[c : c + 1, :] - offset

        @pl.loop(0, ext // tile)
        def _(r):
            start = pl.multiple_of(r * tile, tile)
            node = lax.broadcasted_iota(jnp.int32, (tile, local), 0) + start
            pick_ref[pl.ds(start, tile), c * local : (c + 1) * local] = jnp.where(
                node == named, 1.0, 0.0
            ).astype(BF16)

    greeted = jnp.int32(4 + chips) + (a > 0).astype(jnp.int32) + (a < line - 1).astype(jnp.int32)
    pl.semaphore_wait(barrier, greeted - keeps.astype(jnp.int32))

    def copy(step, side, src, dst):
        return pltpu.make_async_remote_copy(
            src_ref=src, dst_ref=dst, send_sem=ssem.at[step, side], recv_sem=rsem.at[step, 1 - side],
            device_id={"space": to[side]}, device_id_type=MESH_ID,
        )

    flights = [[] for _ in range(DEGREE + 2)]
    flights[0] = [
        copy(0, 0, states_ref.at[:, pl.ds(0, rim)], v_ref.at[0, :, pl.ds(ext - rim, rim)]),
        copy(0, 1, states_ref.at[:, pl.ds(nodes - rim, rim)], v_ref.at[0, :, pl.ds(0, rim)]),
    ]
    for f in flights[0]:
        f.start()

    for c in range(cells):
        named = jnp.transpose(jnp.broadcast_to(conn_ref[c : c + 1, :] - offset, (tile, local)))

        @pl.loop(0, ext // tile)
        def _(n):
            start = pl.multiple_of(n * tile, tile)
            node = lax.broadcasted_iota(jnp.int32, (local, tile), 1) + start
            put_ref[c * local : (c + 1) * local, pl.ds(start, tile)] = jnp.where(
                node == named, 1.0, 0.0
            ).astype(BF16)

    still = jnp.zeros((1, rim), F32)
    pot = jnp.concatenate([still, pot_ref[...], still], axis=1)

    def level(k, image, where):
        held = v_ref[k - 1, :, where].astype(F32)
        if k == 1:
            made = (image - CENTER * held) * (1.0 / HALF)
        else:
            made = (image - CENTER * held) * (2.0 / HALF) - v_ref[k - 2, :, where].astype(F32)
        v_ref[k, :, where] = made.astype(BF16)

    def product(picked):
        return jnp.concatenate(
            [
                jnp.dot(picked[:, c * local : (c + 1) * local], cells_ref[c], preferred_element_type=F32)
                for c in range(cells)
            ],
            axis=1,
        )

    def picked(k, where):
        return jnp.dot(v_ref[k, :, where], pick_ref[where, :], preferred_element_type=F32)

    parts = ((rim, nodes - zone), (0, rim), (nodes - rim, rim))

    def along(way, block, part):
        block = lax.rem(block + line, line)
        spot = col_ref.at[block, :, pl.ds(*parts[part])]
        return pltpu.make_async_remote_copy(
            src_ref=spot, dst_ref=spot, send_sem=lsend.at[way, block, part], recv_sem=lrecv.at[block, part],
            device_id={"state_0": lax.rem(a + line + 2 * way - 1, line)}, device_id_type=MESH_ID,
        )

    def goes(way, hop):
        return (a - hop >= 0) & (a + 1 < line) if way else (a + hop < line) & (a >= 1)

    def come(way, hop):
        return a - hop >= 0 if way else a + hop < line

    def pass_along(hop, part):
        for way in (0, 1):
            block = a - hop if way else a + hop
            if hop:

                @pl.when(come(way, hop))
                def _():
                    along(way, block, part).wait_recv()

            @pl.when(goes(way, hop))
            def _():
                along(way, block, part).start()

    def around(turn, kind, part):
        block = (b, b, beside[0], beside[1])[turn]
        first, count = ((0, rows), (0, rows), (0, half), (half, half))[turn]
        spot = row_ref.at[block, pl.ds(kind * rows + first, count), pl.ds(*parts[part])]
        return pltpu.make_async_remote_copy(
            src_ref=spot, dst_ref=spot, send_sem=wsend.at[turn, kind, part], recv_sem=wrecv.at[turn, kind, part],
            device_id={"state_1": beside[1 - turn % 2]}, device_id_type=MESH_ID,
        )

    def arrive(turn, kind, part):
        block = (beside[0], beside[1], opposite, opposite)[turn]
        first, count = ((0, rows), (0, rows), (0, half), (half, half))[turn]
        spot = row_ref.at[block, pl.ds(kind * rows + first, count), pl.ds(*parts[part])]
        pltpu.make_async_remote_copy(
            src_ref=spot, dst_ref=spot, send_sem=wsend.at[turn, kind, part], recv_sem=wrecv.at[turn, kind, part],
            device_id={"state_1": beside[1 - turn % 2]}, device_id_type=MESH_ID,
        ).wait_recv()

    def send_around(kind, part):
        for turn in (0, 1):
            around(turn, kind, part).start()

    def pass_around(kind, part):
        for turn in (0, 1):
            arrive(turn, kind, part)
            around(turn + 2, kind, part).start()

    def share(part):
        first, count = parts[part]
        own = v_ref[DEGREE, :, rim + first : rim + first + count]
        col_ref[a, :, first : first + count] = own
        row_ref[b, 0:rows, first : first + count] = own
        pass_along(0, part)
        send_around(0, part)

    for k in range(DEGREE + 1):
        acc_ref[...] = product(picked(k, inner).astype(BF16))
        for f in flights[k]:
            f.wait_recv()
        if k:
            for side in (0, 1):
                level(k, part_ref[side] + rcv_ref[k - 1, side].astype(F32), zones[side])
        if k == DEGREE:
            share(1)
            share(2)
        late = (picked(k, zones[0]) + picked(k, zones[1])).astype(BF16)
        products = (acc_ref[...] + product(late)).astype(BF16)

        def image(where):
            placed = jnp.dot(products, put_ref[:, where], preferred_element_type=F32)
            return placed + pot[:, where] * v_ref[k, :, where].astype(F32)

        for side in (0, 1):
            mine = image(zones[side])
            part_ref[side] = mine
            if k < DEGREE:
                snd_ref[k, side] = mine.astype(BF16)
                flights[k + 1].append(copy(k + 1, side, snd_ref.at[k, side], rcv_ref.at[k, 1 - side]))
            else:
                esnd_ref[side] = mine[:, side * rim : (side + 1) * rim].astype(BF16)
                flights[k + 1].append(copy(k + 1, side, esnd_ref.at[side], ercv_ref.at[1 - side]))
            flights[k + 1][-1].start()
        if k < DEGREE:
            level(k + 1, image(inner), inner)
        else:
            filt_ref[...] = v_ref[k, :, rim : rim + nodes]
            row_ref[b, rows : 2 * rows, rim : nodes - rim] = image(inner).astype(BF16)
            send_around(1, 0)
        if k == DEGREE - 1:
            share(0)

    pass_along(1, 0)
    pass_around(0, 0)
    for f in flights[DEGREE + 1]:
        f.wait_recv()
    for side in (0, 1):
        first = side * (nodes - rim)
        own = slice(rim, zone) if side == 0 else slice(0, rim)
        row_ref[b, rows : 2 * rows, first : first + rim] = (
            part_ref[side, :, own] + ercv_ref[side].astype(F32)
        ).astype(BF16)
        send_around(1, 1 + side)
    for part in (1, 2):
        pass_along(1, part)
        pass_around(0, part)
    for hop in range(2, max(line, 3)):
        for part in range(3):
            pass_along(hop, part)
            if hop == 2:
                pass_around(1, part)
    for kind in (0, 1):
        for part in range(3):
            for turn in (2, 3):
                arrive(turn, kind, part)

    broad = prcv_ref.shape[2]

    def to_sibling(i):
        return pltpu.make_async_remote_copy(
            src_ref=csnd_ref.at[i], dst_ref=crcv_ref.at[i], send_sem=csend.at[i], recv_sem=crecv.at[i],
            device_id={"space": sibling}, device_id_type=MESH_ID,
        )

    nearest = chip // wide
    order = [lax.rem(nearest + n, line) for n in range(line)]
    about = [lax.rem(b + n, wide) for n in range(wide)]

    for i in order:
        for j in range(wide):
            block = lax.dot_general(col_ref[i], row_ref[j], TRANSPOSED, preferred_element_type=F32)
            for q in (0, 1):
                top, deep = q * half, half // 2
                sum_ref[i, j, q, 0:half, :] = block[top : top + half, 0:broad]
                sum_ref[i, j, q, half : half + deep, :] = jnp.concatenate(
                    [block[top : top + deep, broad:], block[top + deep : top + half, broad:]], axis=1
                )
            csnd_ref[i, j] = sum_ref[i, j, 1 - core].astype(BF16)
        to_sibling(i).start()

    def to_owner(i, j):
        return pltpu.make_async_remote_copy(
            src_ref=psnd_ref.at[i, j], dst_ref=prcv_ref.at[chip], send_sem=psend.at[i, j], recv_sem=precv.at[chip],
            device_id={"state_1": j, "space": 2 * (i * wide + b) + core}, device_id_type=MESH_ID,
        )

    def stays(i, j):
        return (b == j) & (chip == i * wide + b)

    for i in order:
        to_sibling(i).wait_recv()
        for j in about:
            psnd_ref[i, j] = (sum_ref[i, j, core] + crcv_ref[i, j].astype(F32)).astype(BF16)

            @pl.when(stays(i, j))
            def _():
                prcv_ref[chip] = psnd_ref[i, j]

            @pl.when(jnp.logical_not(stays(i, j)))
            def _():
                to_owner(i, j).start()

    total = jnp.zeros(prcv_ref.shape[1:], F32)
    for p in range(chips):

        @pl.when(jnp.logical_not(keeps & (chip == p)))
        def _():
            pltpu.make_async_remote_copy(
                src_ref=prcv_ref.at[p], dst_ref=prcv_ref.at[p], send_sem=precv.at[p], recv_sem=precv.at[p],
                device_id={"space": sibling}, device_id_type=MESH_ID,
            ).wait_recv()

        total += prcv_ref[p].astype(F32)
    total *= 1.0 / (nodes * ring)
    tail = total[half:]
    tail = jnp.concatenate([tail[:, 0 : broad // 2], tail[:, broad // 2 :]], axis=0)
    inter_ref[...] = total[0:half, 0:rows]
    proj_ref[...] = jnp.concatenate([total[0:half, rows:], tail], axis=1)

    for step in flights:
        for f in step:
            f.wait_send()
    for way in (0, 1):
        for hop in range(line - 1):
            for part in range(3):

                @pl.when(goes(way, hop))
                def _():
                    along(way, a - hop if way else a + hop, part).wait_send()

    for turn in range(4):
        for kind in (0, 1):
            for part in range(3):
                around(turn, kind, part).wait_send()
    for i in range(line):
        to_sibling(i).wait_send()
        for j in range(wide):

            @pl.when(jnp.logical_not(stays(i, j)))
            def _():
                to_owner(i, j).wait_send()


def per_device(states, cell_matrices, connectivity, potential):
    rows, nodes = states.shape
    cells, local, _ = cell_matrices.shape
    line, wide, ring = (lax.axis_size(name) for name in (*STATE, "space"))
    chips, half = ring // 2, rows // 2
    packed = (half + half // 2, 4 * rows // 3)
    rim = local // 4
    ext = nodes + 2 * rim
    vmem = pl.BlockSpec(memory_space=pltpu.VMEM)
    dma = pltpu.SemaphoreType.DMA
    filtered, inter, proj = pl.pallas_call(
        kernel,
        out_shape=(
            jax.ShapeDtypeStruct((rows, nodes), BF16),
            jax.ShapeDtypeStruct((half, rows), F32),
            jax.ShapeDtypeStruct((half, rows), F32),
        ),
        in_specs=[vmem] * 4,
        out_specs=(vmem, vmem, vmem),
        scratch_shapes=[
            pltpu.VMEM((ext, cells * local), BF16),
            pltpu.VMEM((cells * local, ext), BF16),
            pltpu.VMEM((DEGREE + 1, rows, ext), BF16),
            pltpu.VMEM((rows, cells * local), F32),
            pltpu.VMEM((2, rows, 2 * rim), F32),
            pltpu.VMEM((DEGREE, 2, rows, 2 * rim), BF16),
            pltpu.VMEM((DEGREE, 2, rows, 2 * rim), BF16),
            pltpu.VMEM((2, rows, rim), BF16),
            pltpu.VMEM((2, rows, rim), BF16),
            pltpu.VMEM((wide, 2 * rows, nodes), BF16),
            pltpu.VMEM((line, rows, nodes), BF16),
            pltpu.VMEM((line, wide, 2, *packed), F32),
            pltpu.VMEM((line, wide, *packed), BF16),
            pltpu.VMEM((line, wide, *packed), BF16),
            pltpu.VMEM((line, wide, *packed), BF16),
            pltpu.VMEM((chips, *packed), BF16),
            dma((DEGREE + 2, 2)), dma((DEGREE + 2, 2)),
            dma((2, line, 3)), dma((line, 3)),
            dma((4, 2, 3)), dma((4, 2, 3)),
            dma((line,)), dma((line,)),
            dma((line, wide)), dma((chips,)),
        ],
        compiler_params=pltpu.CompilerParams(collective_id=0, has_side_effects=True),
    )(states, cell_matrices, connectivity, potential.reshape(1, -1))
    return filtered, inter.T, proj.T


def solution(mesh):
    line = mesh.shape["state"] // WIDE
    finer = Mesh(mesh.devices.reshape(line, WIDE, mesh.shape["space"]), (*STATE, "space"))
    placed = (P(STATE, "space"), P("space", None, None), P("space", None), P("space"))
    return jax.shard_map(
        per_device,
        mesh=finer,
        in_specs=placed,
        out_specs=(P(STATE, "space"), P(STATE, "space"), P(STATE, "space")),
        check_vma=False,
    )
```

```python
import jax
import jax.numpy as jnp
from jax import lax
from jax.experimental import pallas as pl
from jax.experimental.pallas import tpu as pltpu
from jax.sharding import Mesh
from jax.sharding import PartitionSpec as P

DEGREE = 4
WIDE = 4
GROUPS = 3
STATE = ("state_0", "state_1")
CENTER = 3.0
HALF = 3.5
F32 = jnp.float32
BF16 = jnp.bfloat16
MESH_ID = pl.DeviceIdType.MESH
TRANSPOSED = (((1,), (1,)), ((), ()))


def kernel(
    states_ref, cells_ref, conn_ref, pot_ref,
    filt_ref, inter_ref, proj_ref,
    pick_ref, put_ref, v_ref, acc_ref, potx_ref, near_ref, base_ref,
    part_ref, snd_ref, rcv_ref, esnd_ref, ercv_ref,
    row_ref, col_ref, sum_ref, csnd_ref, crcv_ref, psnd_ref, prcv_ref,
    ssem, rsem, fsend, frecv, lsend, lrecv, wsend, wrecv, csend, crecv, psend, precv,
):
    rows, nodes = states_ref.shape
    cells, local = conn_ref.shape
    ext = pick_ref.shape[0]
    rim = (ext - nodes) // 2
    zone = 2 * rim
    inner = slice(zone, ext - zone)
    half = rows // 2
    ring, line, wide = lax.axis_size("space"), lax.axis_size("state_0"), lax.axis_size("state_1")
    chips = ring // 2
    me, a, b = lax.axis_index("space"), lax.axis_index("state_0"), lax.axis_index("state_1")
    chip, core = me // 2, lax.rem(me, 2)
    to = (lax.rem(me + ring - 1, ring), lax.rem(me + 1, ring))
    beside = (lax.rem(b + wide - 1, wide), lax.rem(b + 1, wide))
    opposite = lax.rem(b + 2, wide)
    sibling = me + 1 - 2 * core
    distant = lax.rem(me + ring - 1 + 2 * core, ring)
    source = lax.rem(chip, wide)
    keeps = b == source

    barrier = pltpu.get_barrier_semaphore()

    def greet(**device):
        pl.semaphore_signal(barrier, inc=1, device_id=device, device_id_type=MESH_ID)

    for side in (0, 1):
        greet(space=to[side])
        greet(state_1=beside[side])

    @pl.when(a > 0)
    def _():
        greet(state_0=a - 1)

    @pl.when(a < line - 1)
    def _():
        greet(state_0=a + 1)

    for p in range(chips):

        @pl.when(jnp.logical_not(keeps & (chip == p)))
        def _():
            greet(state_1=source, space=2 * p + core)

    offset = me * nodes - rim
    v_ref[0, :, rim : rim + nodes] = states_ref[...]

    tile = rim
    for c in range(cells):
        named = conn_ref[c : c + 1, :] - offset

        @pl.loop(0, ext // tile)
        def _(r):
            start = pl.multiple_of(r * tile, tile)
            node = lax.broadcasted_iota(jnp.int32, (tile, local), 0) + start
            pick_ref[pl.ds(start, tile), c * local : (c + 1) * local] = jnp.where(
                node == named, 1.0, 0.0
            ).astype(BF16)

    greeted = jnp.int32(4 + chips) + (a > 0).astype(jnp.int32) + (a < line - 1).astype(jnp.int32)
    pl.semaphore_wait(barrier, greeted - keeps.astype(jnp.int32))

    def lanes(start, width):
        return pl.ds(pl.multiple_of(start, rim), width)

    sign = (core, 1 - core)
    zones = tuple(lanes(n * (ext - zone), zone) for n in sign)
    edges = tuple(n * (nodes - rim) for n in sign)
    outer = tuple(lanes(n * rim, rim) for n in sign)
    own = tuple(lanes((1 - n) * rim, rim) for n in sign)
    groups = tuple(pl.ds(first, rows // GROUPS) for first in range(0, rows, rows // GROUPS))

    def travel(step, side, group):
        if step == 0:
            src = states_ref.at[group, lanes(edges[side], rim)]
            dst = v_ref.at[0, group, lanes((1 - sign[side]) * (ext - rim), rim)]
        elif step <= DEGREE:
            src, dst = snd_ref.at[step - 1, side, group], rcv_ref.at[step - 1, side, group]
        else:
            src, dst = esnd_ref.at[side, group], ercv_ref.at[side, group]
        return src, dst

    def afar(step, g):
        src, dst = travel(step, 0, groups[g])
        return pltpu.make_async_remote_copy(
            src_ref=src, dst_ref=dst, send_sem=ssem.at[step, g], recv_sem=rsem.at[step, g],
            device_id={"space": distant}, device_id_type=MESH_ID,
        )

    def nearby(step):
        src, dst = travel(step, 1, pl.ds(0, rows))
        return pltpu.make_async_remote_copy(
            src_ref=src, dst_ref=dst, send_sem=fsend.at[step], recv_sem=frecv.at[step],
            device_id={"space": sibling}, device_id_type=MESH_ID,
        )

    for g in range(GROUPS):
        afar(0, g).start()
    nearby(0).start()

    for c in range(cells):
        named = jnp.transpose(jnp.broadcast_to(conn_ref[c : c + 1, :] - offset, (tile, local)))

        @pl.loop(0, ext // tile)
        def _(n):
            start = pl.multiple_of(n * tile, tile)
            node = lax.broadcasted_iota(jnp.int32, (local, tile), 1) + start
            put_ref[c * local : (c + 1) * local, pl.ds(start, tile)] = jnp.where(
                node == named, 1.0, 0.0
            ).astype(BF16)

    potx_ref[:, 0:rim] = jnp.zeros((1, rim), F32)
    potx_ref[:, rim : rim + nodes] = pot_ref[...]
    potx_ref[:, ext - rim : ext] = jnp.zeros((1, rim), F32)

    everyone = pl.ds(0, rows)

    def level(k, image, group, where):
        held = v_ref[k - 1, group, where].astype(F32)
        if k == 1:
            made = (image - CENTER * held) * (1.0 / HALF)
        else:
            made = (image - CENTER * held) * (2.0 / HALF) - v_ref[k - 2, group, where].astype(F32)
        v_ref[k, group, where] = made.astype(BF16)

    def product(picked):
        return jnp.concatenate(
            [
                jnp.dot(picked[:, c * local : (c + 1) * local], cells_ref[c], preferred_element_type=F32)
                for c in range(cells)
            ],
            axis=1,
        )

    def picked(k, where):
        return jnp.dot(v_ref[k, :, where], pick_ref[where, :], preferred_element_type=F32).astype(BF16)

    def placed(products, where):
        return jnp.dot(products, put_ref[:, where], preferred_element_type=F32)

    def own_term(k, group, where):
        return potx_ref[:, where] * v_ref[k, group, where].astype(F32)

    through = product(pick_ref[zones[0], :])
    near_ref[0, :, 0 : cells * local] = through.astype(BF16)
    rest = through - near_ref[0, :, 0 : cells * local].astype(F32)
    itself = placed(near_ref[0, :, 0 : cells * local], zones[0]) + placed(rest.astype(BF16), zones[0])
    near_ref[1, :, 0:zone] = itself.astype(BF16)
    near_ref[2, :, 0:zone] = (itself - near_ref[1, :, 0:zone].astype(F32)).astype(BF16)

    parts = ((rim, nodes - zone), (edges[1], rim), (edges[0], rim))

    def along(way, block, part):
        block = lax.rem(block + line, line)
        spot = col_ref.at[block, :, lanes(*parts[part])]
        return pltpu.make_async_remote_copy(
            src_ref=spot, dst_ref=spot, send_sem=lsend.at[way, block, part], recv_sem=lrecv.at[block, part],
            device_id={"state_0": lax.rem(a + line + 2 * way - 1, line)}, device_id_type=MESH_ID,
        )

    def goes(way, hop):
        return (a - hop >= 0) & (a + 1 < line) if way else (a + hop < line) & (a >= 1)

    def come(way, hop):
        return a - hop >= 0 if way else a + hop < line

    def pass_along(hop, part):
        for way in (0, 1):
            block = a - hop if way else a + hop
            if hop:

                @pl.when(come(way, hop))
                def _():
                    along(way, block, part).wait_recv()

            @pl.when(goes(way, hop))
            def _():
                along(way, block, part).start()

    def around(turn, kind, part):
        block = (b, b, beside[0], beside[1])[turn]
        first, count = ((0, rows), (0, rows), (0, half), (half, half))[turn]
        spot = row_ref.at[block, pl.ds(kind * rows + first, count), lanes(*parts[part])]
        return pltpu.make_async_remote_copy(
            src_ref=spot, dst_ref=spot, send_sem=wsend.at[turn, kind, part], recv_sem=wrecv.at[turn, kind, part],
            device_id={"state_1": beside[1 - turn % 2]}, device_id_type=MESH_ID,
        )

    def arrive(turn, kind, part):
        block = (beside[0], beside[1], opposite, opposite)[turn]
        first, count = ((0, rows), (0, rows), (0, half), (half, half))[turn]
        spot = row_ref.at[block, pl.ds(kind * rows + first, count), lanes(*parts[part])]
        pltpu.make_async_remote_copy(
            src_ref=spot, dst_ref=spot, send_sem=wsend.at[turn, kind, part], recv_sem=wrecv.at[turn, kind, part],
            device_id={"state_1": beside[1 - turn % 2]}, device_id_type=MESH_ID,
        ).wait_recv()

    def send_around(kind, part):
        for turn in (0, 1):
            around(turn, kind, part).start()

    def pass_around(kind, part):
        for turn in (0, 1):
            arrive(turn, kind, part)
            around(turn + 2, kind, part).start()

    def share(part):
        first, count = parts[part]
        done = v_ref[DEGREE, :, lanes(rim + first, count)]
        col_ref[a, :, lanes(first, count)] = done
        row_ref[b, 0:rows, lanes(first, count)] = done
        pass_along(0, part)
        send_around(0, part)

    for k in range(DEGREE + 1):
        acc_ref[...] = product(picked(k, inner))
        nearby(k).wait_recv()
        if k:
            level(k, part_ref[1] + rcv_ref[k - 1, 1].astype(F32), everyone, zones[1])
        if k == DEGREE:
            share(1)
        acc_ref[...] += product(picked(k, zones[1]))
        base_ref[...] = placed(acc_ref[...].astype(BF16), zones[0])
        for g, group in enumerate(groups):
            afar(k, g).wait_recv()
            if k:
                level(k, part_ref[0, group, :] + rcv_ref[k - 1, 0, group, :].astype(F32), group, zones[0])
            held = v_ref[k, group, zones[0]]
            mine = base_ref[group, :] + own_term(k, group, zones[0])
            for n in (1, 2):
                mine += jnp.dot(held, near_ref[n, :, 0:zone], preferred_element_type=F32)
            part_ref[0, group, :] = mine
            if k < DEGREE:
                snd_ref[k, 0, group, :] = mine.astype(BF16)
            else:
                esnd_ref[0, group, :] = part_ref[0, group, outer[0]].astype(BF16)
            afar(k + 1, g).start()
        if k == DEGREE:
            share(2)
        products = (acc_ref[...] + product(picked(k, zones[0]))).astype(BF16)
        mine = placed(products, zones[1]) + own_term(k, everyone, zones[1])
        part_ref[1] = mine
        if k < DEGREE:
            snd_ref[k, 1] = mine.astype(BF16)
        else:
            esnd_ref[1] = part_ref[1, :, outer[1]].astype(BF16)
        nearby(k + 1).start()
        mine = placed(products, inner) + own_term(k, everyone, inner)
        if k < DEGREE:
            level(k + 1, mine, everyone, inner)
        else:
            filt_ref[...] = v_ref[k, :, rim : rim + nodes]
            row_ref[b, rows : 2 * rows, rim : nodes - rim] = mine.astype(BF16)
            send_around(1, 0)
        if k == DEGREE - 1:
            share(0)

    def energy(side):
        row_ref[b, rows : 2 * rows, lanes(edges[side], rim)] = (
            part_ref[side, :, own[side]] + ercv_ref[side].astype(F32)
        ).astype(BF16)

    nearby(DEGREE + 1).wait_recv()
    energy(1)
    send_around(1, 1)
    pass_along(1, 0)
    pass_around(0, 0)
    for g in range(GROUPS):
        afar(DEGREE + 1, g).wait_recv()
    energy(0)
    send_around(1, 2)
    for part in (1, 2):
        pass_along(1, part)
        pass_around(0, part)
    for hop in range(2, max(line, 3)):
        for part in range(3):
            pass_along(hop, part)
            if hop == 2:
                pass_around(1, part)
    for kind in (0, 1):
        for part in range(3):
            for turn in (2, 3):
                arrive(turn, kind, part)

    broad = prcv_ref.shape[2]

    def to_sibling(i):
        return pltpu.make_async_remote_copy(
            src_ref=csnd_ref.at[i], dst_ref=crcv_ref.at[i], send_sem=csend.at[i], recv_sem=crecv.at[i],
            device_id={"space": sibling}, device_id_type=MESH_ID,
        )

    nearest = chip // wide
    order = [lax.rem(nearest + n, line) for n in range(line)]
    about = [lax.rem(b + n, wide) for n in range(wide)]

    for i in order:
        for j in range(wide):
            block = lax.dot_general(col_ref[i], row_ref[j], TRANSPOSED, preferred_element_type=F32)
            for q in (0, 1):
                top, deep = q * half, half // 2
                sum_ref[i, j, q, 0:half, :] = block[top : top + half, 0:broad]
                sum_ref[i, j, q, half : half + deep, :] = jnp.concatenate(
                    [block[top : top + deep, broad:], block[top + deep : top + half, broad:]], axis=1
                )
            csnd_ref[i, j] = sum_ref[i, j, 1 - core].astype(BF16)
        to_sibling(i).start()

    def to_owner(i, j):
        return pltpu.make_async_remote_copy(
            src_ref=psnd_ref.at[i, j], dst_ref=prcv_ref.at[chip], send_sem=psend.at[i, j], recv_sem=precv.at[chip],
            device_id={"state_1": j, "space": 2 * (i * wide + b) + core}, device_id_type=MESH_ID,
        )

    def stays(i, j):
        return (b == j) & (chip == i * wide + b)

    for i in order:
        to_sibling(i).wait_recv()
        for j in about:
            psnd_ref[i, j] = (sum_ref[i, j, core] + crcv_ref[i, j].astype(F32)).astype(BF16)

            @pl.when(stays(i, j))
            def _():
                prcv_ref[chip] = psnd_ref[i, j]

            @pl.when(jnp.logical_not(stays(i, j)))
            def _():
                to_owner(i, j).start()

    total = jnp.zeros(prcv_ref.shape[1:], F32)
    for p in range(chips):

        @pl.when(jnp.logical_not(keeps & (chip == p)))
        def _():
            pltpu.make_async_remote_copy(
                src_ref=prcv_ref.at[p], dst_ref=prcv_ref.at[p], send_sem=precv.at[p], recv_sem=precv.at[p],
                device_id={"space": sibling}, device_id_type=MESH_ID,
            ).wait_recv()

        total += prcv_ref[p].astype(F32)
    total *= 1.0 / (nodes * ring)
    tail = total[half:]
    tail = jnp.concatenate([tail[:, 0 : broad // 2], tail[:, broad // 2 :]], axis=0)
    inter_ref[...] = total[0:half, 0:rows]
    proj_ref[...] = jnp.concatenate([total[0:half, rows:], tail], axis=1)

    for step in range(DEGREE + 2):
        nearby(step).wait_send()
        for g in range(GROUPS):
            afar(step, g).wait_send()
    for way in (0, 1):
        for hop in range(line - 1):
            for part in range(3):

                @pl.when(goes(way, hop))
                def _():
                    along(way, a - hop if way else a + hop, part).wait_send()

    for turn in range(4):
        for kind in (0, 1):
            for part in range(3):
                around(turn, kind, part).wait_send()
    for i in range(line):
        to_sibling(i).wait_send()
        for j in range(wide):

            @pl.when(jnp.logical_not(stays(i, j)))
            def _():
                to_owner(i, j).wait_send()


def per_device(states, cell_matrices, connectivity, potential):
    rows, nodes = states.shape
    cells, local, _ = cell_matrices.shape
    line, wide, ring = (lax.axis_size(name) for name in (*STATE, "space"))
    chips, half = ring // 2, rows // 2
    packed = (half + half // 2, 4 * rows // 3)
    rim = local // 4
    ext = nodes + 2 * rim
    vmem = pl.BlockSpec(memory_space=pltpu.VMEM)
    dma = pltpu.SemaphoreType.DMA
    filtered, inter, proj = pl.pallas_call(
        kernel,
        out_shape=(
            jax.ShapeDtypeStruct((rows, nodes), BF16),
            jax.ShapeDtypeStruct((half, rows), F32),
            jax.ShapeDtypeStruct((half, rows), F32),
        ),
        in_specs=[vmem] * 4,
        out_specs=(vmem, vmem, vmem),
        scratch_shapes=[
            pltpu.VMEM((ext, cells * local), BF16),
            pltpu.VMEM((cells * local, ext), BF16),
            pltpu.VMEM((DEGREE + 1, rows, ext), BF16),
            pltpu.VMEM((rows, cells * local), F32),
            pltpu.VMEM((1, ext), F32),
            pltpu.VMEM((3, 2 * rim, cells * local), BF16),
            pltpu.VMEM((rows, 2 * rim), F32),
            pltpu.VMEM((2, rows, 2 * rim), F32),
            pltpu.VMEM((DEGREE, 2, rows, 2 * rim), BF16),
            pltpu.VMEM((DEGREE, 2, rows, 2 * rim), BF16),
            pltpu.VMEM((2, rows, rim), BF16),
            pltpu.VMEM((2, rows, rim), BF16),
            pltpu.VMEM((wide, 2 * rows, nodes), BF16),
            pltpu.VMEM((line, rows, nodes), BF16),
            pltpu.VMEM((line, wide, 2, *packed), F32),
            pltpu.VMEM((line, wide, *packed), BF16),
            pltpu.VMEM((line, wide, *packed), BF16),
            pltpu.VMEM((line, wide, *packed), BF16),
            pltpu.VMEM((chips, *packed), BF16),
            dma((DEGREE + 2, GROUPS)), dma((DEGREE + 2, GROUPS)),
            dma((DEGREE + 2,)), dma((DEGREE + 2,)),
            dma((2, line, 3)), dma((line, 3)),
            dma((4, 2, 3)), dma((4, 2, 3)),
            dma((line,)), dma((line,)),
            dma((line, wide)), dma((chips,)),
        ],
        compiler_params=pltpu.CompilerParams(collective_id=0, has_side_effects=True),
    )(states, cell_matrices, connectivity, potential.reshape(1, -1))
    return filtered, inter.T, proj.T


def solution(mesh):
    line = mesh.shape["state"] // WIDE
    finer = Mesh(mesh.devices.reshape(line, WIDE, mesh.shape["space"]), (*STATE, "space"))
    placed = (P(STATE, "space"), P("space", None, None), P("space", None), P("space"))
    return jax.shard_map(
        per_device,
        mesh=finer,
        in_specs=placed,
        out_specs=(P(STATE, "space"), P(STATE, "space"), P(STATE, "space")),
        check_vma=False,
    )
```

```python
import jax
import jax.numpy as jnp
from jax import lax
from jax.experimental import pallas as pl
from jax.experimental.pallas import tpu as pltpu
from jax.sharding import Mesh
from jax.sharding import PartitionSpec as P

DEGREE = 4
WIDE = 4
GROUPS = 3
PIECES = 2
STATE = ("state_0", "state_1")
CENTER = 3.0
HALF = 3.5
F32 = jnp.float32
BF16 = jnp.bfloat16
MESH_ID = pl.DeviceIdType.MESH
TRANSPOSED = (((1,), (1,)), ((), ()))


def kernel(
    states_ref, cells_ref, conn_ref, pot_ref,
    filt_ref, inter_ref, proj_ref,
    pick_ref, put_ref, v_ref, acc_ref, potx_ref, near_ref, base_ref,
    part_ref, snd_ref, rcv_ref, esnd_ref, ercv_ref,
    row_ref, col_ref, sum_ref, csnd_ref, crcv_ref, psnd_ref, prcv_ref,
    ssem, rsem, fsend, frecv, lsend, lrecv, wsend, wrecv, csend, crecv, psend, precv,
):
    rows, nodes = states_ref.shape
    cells, local = conn_ref.shape
    ext = pick_ref.shape[0]
    rim = (ext - nodes) // 2
    zone = 2 * rim
    inner = slice(zone, ext - zone)
    half = rows // 2
    ring, line, wide = lax.axis_size("space"), lax.axis_size("state_0"), lax.axis_size("state_1")
    chips = ring // 2
    me, a, b = lax.axis_index("space"), lax.axis_index("state_0"), lax.axis_index("state_1")
    chip, core = me // 2, lax.rem(me, 2)
    to = (lax.rem(me + ring - 1, ring), lax.rem(me + 1, ring))
    beside = (lax.rem(b + wide - 1, wide), lax.rem(b + 1, wide))
    opposite = lax.rem(b + 2, wide)
    sibling = me + 1 - 2 * core
    distant = lax.rem(me + ring - 1 + 2 * core, ring)
    source = lax.rem(chip, wide)
    keeps = b == source

    barrier = pltpu.get_barrier_semaphore()

    def greet(**device):
        pl.semaphore_signal(barrier, inc=1, device_id=device, device_id_type=MESH_ID)

    for side in (0, 1):
        greet(space=to[side])
        greet(state_1=beside[side])

    @pl.when(a > 0)
    def _():
        greet(state_0=a - 1)

    @pl.when(a < line - 1)
    def _():
        greet(state_0=a + 1)

    for p in range(chips):

        @pl.when(jnp.logical_not(keeps & (chip == p)))
        def _():
            greet(state_1=source, space=2 * p + core)

    offset = me * nodes - rim
    v_ref[0, :, rim : rim + nodes] = states_ref[...]

    tile = rim
    for c in range(cells):
        named = conn_ref[c : c + 1, :] - offset

        @pl.loop(0, ext // tile)
        def _(r):
            start = pl.multiple_of(r * tile, tile)
            node = lax.broadcasted_iota(jnp.int32, (tile, local), 0) + start
            pick_ref[pl.ds(start, tile), c * local : (c + 1) * local] = jnp.where(
                node == named, 1.0, 0.0
            ).astype(BF16)

    greeted = jnp.int32(4 + chips) + (a > 0).astype(jnp.int32) + (a < line - 1).astype(jnp.int32)
    pl.semaphore_wait(barrier, greeted - keeps.astype(jnp.int32))

    def lanes(start, width):
        return pl.ds(pl.multiple_of(start, rim), width)

    sign = (core, 1 - core)
    zones = tuple(lanes(n * (ext - zone), zone) for n in sign)
    edges = tuple(n * (nodes - rim) for n in sign)
    outer = tuple(lanes(n * rim, rim) for n in sign)
    own = tuple(lanes((1 - n) * rim, rim) for n in sign)
    groups = tuple(pl.ds(first, rows // GROUPS) for first in range(0, rows, rows // GROUPS))

    def travel(step, side, group):
        if step == 0:
            src = states_ref.at[group, lanes(edges[side], rim)]
            dst = v_ref.at[0, group, lanes((1 - sign[side]) * (ext - rim), rim)]
        elif step <= DEGREE:
            src, dst = snd_ref.at[step - 1, side, group], rcv_ref.at[step - 1, side, group]
        else:
            src, dst = esnd_ref.at[side, group], ercv_ref.at[side, group]
        return src, dst

    def afar(step, g):
        src, dst = travel(step, 0, groups[g])
        return pltpu.make_async_remote_copy(
            src_ref=src, dst_ref=dst, send_sem=ssem.at[step, g], recv_sem=rsem.at[step, g],
            device_id={"space": distant}, device_id_type=MESH_ID,
        )

    def nearby(step):
        src, dst = travel(step, 1, pl.ds(0, rows))
        return pltpu.make_async_remote_copy(
            src_ref=src, dst_ref=dst, send_sem=fsend.at[step], recv_sem=frecv.at[step],
            device_id={"space": sibling}, device_id_type=MESH_ID,
        )

    for g in range(GROUPS):
        afar(0, g).start()
    nearby(0).start()

    for c in range(cells):
        named = jnp.transpose(jnp.broadcast_to(conn_ref[c : c + 1, :] - offset, (tile, local)))

        @pl.loop(0, ext // tile)
        def _(n):
            start = pl.multiple_of(n * tile, tile)
            node = lax.broadcasted_iota(jnp.int32, (local, tile), 1) + start
            put_ref[c * local : (c + 1) * local, pl.ds(start, tile)] = jnp.where(
                node == named, 1.0, 0.0
            ).astype(BF16)

    potx_ref[:, 0:rim] = jnp.zeros((1, rim), F32)
    potx_ref[:, rim : rim + nodes] = pot_ref[...]
    potx_ref[:, ext - rim : ext] = jnp.zeros((1, rim), F32)

    everyone = pl.ds(0, rows)

    def level(k, image, group, where):
        held = v_ref[k - 1, group, where].astype(F32)
        if k == 1:
            made = (image - CENTER * held) * (1.0 / HALF)
        else:
            made = (image - CENTER * held) * (2.0 / HALF) - v_ref[k - 2, group, where].astype(F32)
        v_ref[k, group, where] = made.astype(BF16)

    def product(picked):
        return jnp.concatenate(
            [
                jnp.dot(picked[:, c * local : (c + 1) * local], cells_ref[c], preferred_element_type=F32)
                for c in range(cells)
            ],
            axis=1,
        )

    def picked(k, where):
        return jnp.dot(v_ref[k, :, where], pick_ref[where, :], preferred_element_type=F32).astype(BF16)

    def placed(products, where):
        return jnp.dot(products, put_ref[:, where], preferred_element_type=F32)

    def own_term(k, group, where):
        return potx_ref[:, where] * v_ref[k, group, where].astype(F32)

    through = product(pick_ref[zones[0], :])
    near_ref[0, :, 0 : cells * local] = through.astype(BF16)
    rest = through - near_ref[0, :, 0 : cells * local].astype(F32)
    itself = placed(near_ref[0, :, 0 : cells * local], zones[0]) + placed(rest.astype(BF16), zones[0])
    near_ref[1, :, 0:zone] = itself.astype(BF16)
    near_ref[2, :, 0:zone] = (itself - near_ref[1, :, 0:zone].astype(F32)).astype(BF16)

    piece = (nodes - zone) // PIECES
    early = range(PIECES)
    near, far = PIECES, PIECES + 1
    parts = (*((rim + n * piece, piece) for n in early), (edges[1], rim), (edges[0], rim))

    def along(way, block, part):
        block = lax.rem(block + line, line)
        spot = col_ref.at[block, :, lanes(*parts[part])]
        return pltpu.make_async_remote_copy(
            src_ref=spot, dst_ref=spot, send_sem=lsend.at[way, block, part], recv_sem=lrecv.at[block, part],
            device_id={"state_0": lax.rem(a + line + 2 * way - 1, line)}, device_id_type=MESH_ID,
        )

    def goes(way, hop):
        return (a - hop >= 0) & (a + 1 < line) if way else (a + hop < line) & (a >= 1)

    def come(way, hop):
        return a - hop >= 0 if way else a + hop < line

    def pass_along(hop, part):
        for way in (0, 1):
            block = a - hop if way else a + hop
            if hop:

                @pl.when(come(way, hop))
                def _():
                    along(way, block, part).wait_recv()

            @pl.when(goes(way, hop))
            def _():
                along(way, block, part).start()

    def around(turn, kind, part):
        block = (b, b, beside[0], beside[1])[turn]
        first, count = ((0, rows), (0, rows), (0, half), (half, half))[turn]
        spot = row_ref.at[block, pl.ds(kind * rows + first, count), lanes(*parts[part])]
        return pltpu.make_async_remote_copy(
            src_ref=spot, dst_ref=spot, send_sem=wsend.at[turn, kind, part], recv_sem=wrecv.at[turn, kind, part],
            device_id={"state_1": beside[1 - turn % 2]}, device_id_type=MESH_ID,
        )

    def arrive(turn, kind, part):
        block = (beside[0], beside[1], opposite, opposite)[turn]
        first, count = ((0, rows), (0, rows), (0, half), (half, half))[turn]
        spot = row_ref.at[block, pl.ds(kind * rows + first, count), lanes(*parts[part])]
        pltpu.make_async_remote_copy(
            src_ref=spot, dst_ref=spot, send_sem=wsend.at[turn, kind, part], recv_sem=wrecv.at[turn, kind, part],
            device_id={"state_1": beside[1 - turn % 2]}, device_id_type=MESH_ID,
        ).wait_recv()

    def send_around(kind, part):
        for turn in (0, 1):
            around(turn, kind, part).start()

    def pass_around(kind, part):
        for turn in (0, 1):
            arrive(turn, kind, part)
            around(turn + 2, kind, part).start()

    def share(part):
        first, count = parts[part]
        done = v_ref[DEGREE, :, lanes(rim + first, count)]
        col_ref[a, :, lanes(first, count)] = done
        row_ref[b, 0:rows, lanes(first, count)] = done
        pass_along(0, part)
        send_around(0, part)

    for k in range(DEGREE + 1):
        acc_ref[...] = product(picked(k, inner))
        nearby(k).wait_recv()
        if k:
            level(k, part_ref[1] + rcv_ref[k - 1, 1].astype(F32), everyone, zones[1])
        if k == DEGREE:
            share(near)
        acc_ref[...] += product(picked(k, zones[1]))
        base_ref[...] = placed(acc_ref[...].astype(BF16), zones[0])
        if k == DEGREE:
            for part in early:
                pass_along(1, part)
                pass_around(0, part)
        for g, group in enumerate(groups):
            afar(k, g).wait_recv()
            if k:
                level(k, part_ref[0, group, :] + rcv_ref[k - 1, 0, group, :].astype(F32), group, zones[0])
            held = v_ref[k, group, zones[0]]
            mine = base_ref[group, :] + own_term(k, group, zones[0])
            for n in (1, 2):
                mine += jnp.dot(held, near_ref[n, :, 0:zone], preferred_element_type=F32)
            part_ref[0, group, :] = mine
            if k < DEGREE:
                snd_ref[k, 0, group, :] = mine.astype(BF16)
            else:
                esnd_ref[0, group, :] = part_ref[0, group, outer[0]].astype(BF16)
            afar(k + 1, g).start()
        if k == DEGREE:
            share(far)
        products = (acc_ref[...] + product(picked(k, zones[0]))).astype(BF16)
        mine = placed(products, zones[1]) + own_term(k, everyone, zones[1])
        part_ref[1] = mine
        if k < DEGREE:
            snd_ref[k, 1] = mine.astype(BF16)
        else:
            esnd_ref[1] = part_ref[1, :, outer[1]].astype(BF16)
        nearby(k + 1).start()
        mine = placed(products, inner) + own_term(k, everyone, inner)
        if k < DEGREE:
            level(k + 1, mine, everyone, inner)
        else:
            filt_ref[...] = v_ref[k, :, rim : rim + nodes]
            row_ref[b, rows : 2 * rows, rim : nodes - rim] = mine.astype(BF16)
            for part in early:
                send_around(1, part)
        if k == DEGREE - 1:
            for part in early:
                share(part)

    def energy(side):
        row_ref[b, rows : 2 * rows, lanes(edges[side], rim)] = (
            part_ref[side, :, own[side]] + ercv_ref[side].astype(F32)
        ).astype(BF16)

    nearby(DEGREE + 1).wait_recv()
    energy(1)
    send_around(1, near)
    pass_along(1, near)
    pass_around(0, near)
    for part in early:
        pass_along(2, part)
    pass_along(1, far)
    pass_around(0, far)
    for part in early:
        pass_around(1, part)
    pass_along(2, near)
    pass_around(1, near)
    pass_along(2, far)
    for g in range(GROUPS):
        afar(DEGREE + 1, g).wait_recv()
    energy(0)
    send_around(1, far)
    pass_around(1, far)
    for hop in range(3, line):
        for part in range(len(parts)):
            pass_along(hop, part)
    for kind in (0, 1):
        for part in range(len(parts)):
            for turn in (2, 3):
                arrive(turn, kind, part)

    broad = prcv_ref.shape[2]

    def to_sibling(i):
        return pltpu.make_async_remote_copy(
            src_ref=csnd_ref.at[i], dst_ref=crcv_ref.at[i], send_sem=csend.at[i], recv_sem=crecv.at[i],
            device_id={"space": sibling}, device_id_type=MESH_ID,
        )

    nearest = chip // wide
    order = [lax.rem(nearest + n, line) for n in range(line)]
    about = [lax.rem(b + n, wide) for n in range(wide)]

    for i in order:
        for j in range(wide):
            block = lax.dot_general(col_ref[i], row_ref[j], TRANSPOSED, preferred_element_type=F32)
            for q in (0, 1):
                top, deep = q * half, half // 2
                sum_ref[i, j, q, 0:half, :] = block[top : top + half, 0:broad]
                sum_ref[i, j, q, half : half + deep, :] = jnp.concatenate(
                    [block[top : top + deep, broad:], block[top + deep : top + half, broad:]], axis=1
                )
            csnd_ref[i, j] = sum_ref[i, j, 1 - core].astype(BF16)
        to_sibling(i).start()

    def to_owner(i, j):
        return pltpu.make_async_remote_copy(
            src_ref=psnd_ref.at[i, j], dst_ref=prcv_ref.at[chip], send_sem=psend.at[i, j], recv_sem=precv.at[chip],
            device_id={"state_1": j, "space": 2 * (i * wide + b) + core}, device_id_type=MESH_ID,
        )

    def stays(i, j):
        return (b == j) & (chip == i * wide + b)

    for i in order:
        to_sibling(i).wait_recv()
        for j in about:
            psnd_ref[i, j] = (sum_ref[i, j, core] + crcv_ref[i, j].astype(F32)).astype(BF16)

            @pl.when(stays(i, j))
            def _():
                prcv_ref[chip] = psnd_ref[i, j]

            @pl.when(jnp.logical_not(stays(i, j)))
            def _():
                to_owner(i, j).start()

    total = jnp.zeros(prcv_ref.shape[1:], F32)
    for p in range(chips):

        @pl.when(jnp.logical_not(keeps & (chip == p)))
        def _():
            pltpu.make_async_remote_copy(
                src_ref=prcv_ref.at[p], dst_ref=prcv_ref.at[p], send_sem=precv.at[p], recv_sem=precv.at[p],
                device_id={"space": sibling}, device_id_type=MESH_ID,
            ).wait_recv()

        total += prcv_ref[p].astype(F32)
    total *= 1.0 / (nodes * ring)
    tail = total[half:]
    tail = jnp.concatenate([tail[:, 0 : broad // 2], tail[:, broad // 2 :]], axis=0)
    inter_ref[...] = total[0:half, 0:rows]
    proj_ref[...] = jnp.concatenate([total[0:half, rows:], tail], axis=1)

    for step in range(DEGREE + 2):
        nearby(step).wait_send()
        for g in range(GROUPS):
            afar(step, g).wait_send()
    for way in (0, 1):
        for hop in range(line - 1):
            for part in range(len(parts)):

                @pl.when(goes(way, hop))
                def _():
                    along(way, a - hop if way else a + hop, part).wait_send()

    for turn in range(4):
        for kind in (0, 1):
            for part in range(len(parts)):
                around(turn, kind, part).wait_send()
    for i in range(line):
        to_sibling(i).wait_send()
        for j in range(wide):

            @pl.when(jnp.logical_not(stays(i, j)))
            def _():
                to_owner(i, j).wait_send()


def per_device(states, cell_matrices, connectivity, potential):
    rows, nodes = states.shape
    cells, local, _ = cell_matrices.shape
    line, wide, ring = (lax.axis_size(name) for name in (*STATE, "space"))
    chips, half = ring // 2, rows // 2
    packed = (half + half // 2, 4 * rows // 3)
    rim = local // 4
    ext = nodes + 2 * rim
    vmem = pl.BlockSpec(memory_space=pltpu.VMEM)
    dma = pltpu.SemaphoreType.DMA
    filtered, inter, proj = pl.pallas_call(
        kernel,
        out_shape=(
            jax.ShapeDtypeStruct((rows, nodes), BF16),
            jax.ShapeDtypeStruct((half, rows), F32),
            jax.ShapeDtypeStruct((half, rows), F32),
        ),
        in_specs=[vmem] * 4,
        out_specs=(vmem, vmem, vmem),
        scratch_shapes=[
            pltpu.VMEM((ext, cells * local), BF16),
            pltpu.VMEM((cells * local, ext), BF16),
            pltpu.VMEM((DEGREE + 1, rows, ext), BF16),
            pltpu.VMEM((rows, cells * local), F32),
            pltpu.VMEM((1, ext), F32),
            pltpu.VMEM((3, 2 * rim, cells * local), BF16),
            pltpu.VMEM((rows, 2 * rim), F32),
            pltpu.VMEM((2, rows, 2 * rim), F32),
            pltpu.VMEM((DEGREE, 2, rows, 2 * rim), BF16),
            pltpu.VMEM((DEGREE, 2, rows, 2 * rim), BF16),
            pltpu.VMEM((2, rows, rim), BF16),
            pltpu.VMEM((2, rows, rim), BF16),
            pltpu.VMEM((wide, 2 * rows, nodes), BF16),
            pltpu.VMEM((line, rows, nodes), BF16),
            pltpu.VMEM((line, wide, 2, *packed), F32),
            pltpu.VMEM((line, wide, *packed), BF16),
            pltpu.VMEM((line, wide, *packed), BF16),
            pltpu.VMEM((line, wide, *packed), BF16),
            pltpu.VMEM((chips, *packed), BF16),
            dma((DEGREE + 2, GROUPS)), dma((DEGREE + 2, GROUPS)),
            dma((DEGREE + 2,)), dma((DEGREE + 2,)),
            dma((2, line, PIECES + 2)), dma((line, PIECES + 2)),
            dma((4, 2, PIECES + 2)), dma((4, 2, PIECES + 2)),
            dma((line,)), dma((line,)),
            dma((line, wide)), dma((chips,)),
        ],
        compiler_params=pltpu.CompilerParams(collective_id=0, has_side_effects=True),
    )(states, cell_matrices, connectivity, potential.reshape(1, -1))
    return filtered, inter.T, proj.T


def solution(mesh):
    line = mesh.shape["state"] // WIDE
    finer = Mesh(mesh.devices.reshape(line, WIDE, mesh.shape["space"]), (*STATE, "space"))
    placed = (P(STATE, "space"), P("space", None, None), P("space", None), P("space"))
    return jax.shard_map(
        per_device,
        mesh=finer,
        in_specs=placed,
        out_specs=(P(STATE, "space"), P(STATE, "space"), P(STATE, "space")),
        check_vma=False,
    )
```

```python
import jax
import jax.numpy as jnp
from jax import lax
from jax.experimental import pallas as pl
from jax.experimental.pallas import tpu as pltpu
from jax.sharding import Mesh
from jax.sharding import PartitionSpec as P

DEGREE = 4
WIDE = 4
GROUPS = 3
PIECES = 2
STATE = ("state_0", "state_1")
CENTER = 3.0
HALF = 3.5
F32 = jnp.float32
BF16 = jnp.bfloat16
MESH_ID = pl.DeviceIdType.MESH
TRANSPOSED = (((1,), (1,)), ((), ()))


def kernel(
    states_ref, cells_ref, conn_ref, pot_ref,
    filt_ref, inter_ref, proj_ref,
    pick_ref, put_ref, v_ref, acc_ref, potx_ref, near_ref, base_ref,
    part_ref, snd_ref, rcv_ref, esnd_ref, ercv_ref,
    row_ref, col_ref, sum_ref, csnd_ref, crcv_ref, psnd_ref, prcv_ref,
    ssem, rsem, fsend, frecv, lsend, lrecv, wsend, wrecv, csend, crecv, psend, precv,
):
    rows, nodes = states_ref.shape
    cells, local = conn_ref.shape
    ext = pick_ref.shape[0]
    rim = (ext - nodes) // 2
    zone = 2 * rim
    inner = slice(zone, ext - zone)
    half = rows // 2
    ring, line, wide = lax.axis_size("space"), lax.axis_size("state_0"), lax.axis_size("state_1")
    chips = ring // 2
    me, a, b = lax.axis_index("space"), lax.axis_index("state_0"), lax.axis_index("state_1")
    chip, core = me // 2, lax.rem(me, 2)
    to = (lax.rem(me + ring - 1, ring), lax.rem(me + 1, ring))
    beside = (lax.rem(b + wide - 1, wide), lax.rem(b + 1, wide))
    opposite = lax.rem(b + 2, wide)
    sibling = me + 1 - 2 * core
    distant = lax.rem(me + ring - 1 + 2 * core, ring)
    source = lax.rem(chip, wide)
    keeps = b == source

    barrier = pltpu.get_barrier_semaphore()

    def greet(**device):
        pl.semaphore_signal(barrier, inc=1, device_id=device, device_id_type=MESH_ID)

    for side in (0, 1):
        greet(space=to[side])
        greet(state_1=beside[side])

    @pl.when(a > 0)
    def _():
        greet(state_0=a - 1)

    @pl.when(a < line - 1)
    def _():
        greet(state_0=a + 1)

    for p in range(chips):

        @pl.when(jnp.logical_not(keeps & (chip == p)))
        def _():
            greet(state_1=source, space=2 * p + core)

    offset = me * nodes - rim
    v_ref[0, :, rim : rim + nodes] = states_ref[...]

    tile = rim
    for c in range(cells):
        named = conn_ref[c : c + 1, :] - offset

        @pl.loop(0, ext // tile)
        def _(r):
            start = pl.multiple_of(r * tile, tile)
            node = lax.broadcasted_iota(jnp.int32, (tile, local), 0) + start
            pick_ref[pl.ds(start, tile), c * local : (c + 1) * local] = jnp.where(
                node == named, 1.0, 0.0
            ).astype(BF16)

    greeted = jnp.int32(4 + chips) + (a > 0).astype(jnp.int32) + (a < line - 1).astype(jnp.int32)
    pl.semaphore_wait(barrier, greeted - keeps.astype(jnp.int32))

    def lanes(start, width):
        return pl.ds(pl.multiple_of(start, rim), width)

    sign = (core, 1 - core)
    zones = tuple(lanes(n * (ext - zone), zone) for n in sign)
    edges = tuple(n * (nodes - rim) for n in sign)
    outer = tuple(lanes(n * rim, rim) for n in sign)
    own = tuple(lanes((1 - n) * rim, rim) for n in sign)
    groups = tuple(pl.ds(first, rows // GROUPS) for first in range(0, rows, rows // GROUPS))

    def travel(step, side, group):
        if step == 0:
            src = states_ref.at[group, lanes(edges[side], rim)]
            dst = v_ref.at[0, group, lanes((1 - sign[side]) * (ext - rim), rim)]
        elif step <= DEGREE:
            src, dst = snd_ref.at[step - 1, side, group], rcv_ref.at[step - 1, side, group]
        else:
            src, dst = esnd_ref.at[side, group], ercv_ref.at[side, group]
        return src, dst

    def afar(step, g):
        src, dst = travel(step, 0, groups[g])
        return pltpu.make_async_remote_copy(
            src_ref=src, dst_ref=dst, send_sem=ssem.at[step, g], recv_sem=rsem.at[step, g],
            device_id={"space": distant}, device_id_type=MESH_ID,
        )

    def nearby(step):
        src, dst = travel(step, 1, pl.ds(0, rows))
        return pltpu.make_async_remote_copy(
            src_ref=src, dst_ref=dst, send_sem=fsend.at[step], recv_sem=frecv.at[step],
            device_id={"space": sibling}, device_id_type=MESH_ID,
        )

    for g in range(GROUPS):
        afar(0, g).start()
    nearby(0).start()

    for c in range(cells):
        named = jnp.transpose(jnp.broadcast_to(conn_ref[c : c + 1, :] - offset, (tile, local)))

        @pl.loop(0, ext // tile)
        def _(n):
            start = pl.multiple_of(n * tile, tile)
            node = lax.broadcasted_iota(jnp.int32, (local, tile), 1) + start
            put_ref[c * local : (c + 1) * local, pl.ds(start, tile)] = jnp.where(
                node == named, 1.0, 0.0
            ).astype(BF16)

    potx_ref[:, 0:rim] = jnp.zeros((1, rim), F32)
    potx_ref[:, rim : rim + nodes] = pot_ref[...]
    potx_ref[:, ext - rim : ext] = jnp.zeros((1, rim), F32)

    everyone = pl.ds(0, rows)

    def level(k, image, group, where):
        held = v_ref[k - 1, group, where].astype(F32)
        if k == 1:
            made = (image - CENTER * held) * (1.0 / HALF)
        else:
            made = (image - CENTER * held) * (2.0 / HALF) - v_ref[k - 2, group, where].astype(F32)
        v_ref[k, group, where] = made.astype(BF16)

    def product(picked):
        return jnp.concatenate(
            [
                jnp.dot(picked[:, c * local : (c + 1) * local], cells_ref[c], preferred_element_type=F32)
                for c in range(cells)
            ],
            axis=1,
        )

    def picked(k, where):
        return jnp.dot(v_ref[k, :, where], pick_ref[where, :], preferred_element_type=F32).astype(BF16)

    def placed(products, where):
        return jnp.dot(products, put_ref[:, where], preferred_element_type=F32)

    def own_term(k, group, where):
        return potx_ref[:, where] * v_ref[k, group, where].astype(F32)

    through = product(pick_ref[zones[0], :])
    near_ref[0, :, 0 : cells * local] = through.astype(BF16)
    rest = through - near_ref[0, :, 0 : cells * local].astype(F32)
    itself = placed(near_ref[0, :, 0 : cells * local], zones[0]) + placed(rest.astype(BF16), zones[0])
    near_ref[1, :, 0:zone] = itself.astype(BF16)
    near_ref[2, :, 0:zone] = (itself - near_ref[1, :, 0:zone].astype(F32)).astype(BF16)

    piece = (nodes - zone) // PIECES
    early = range(PIECES)
    near, far = PIECES, PIECES + 1
    parts = (*((rim + n * piece, piece) for n in early), (edges[1], rim), (edges[0], rim))

    def along(way, block, part):
        block = lax.rem(block + line, line)
        spot = col_ref.at[block, :, lanes(*parts[part])]
        return pltpu.make_async_remote_copy(
            src_ref=spot, dst_ref=spot, send_sem=lsend.at[way, block, part], recv_sem=lrecv.at[block, part],
            device_id={"state_0": lax.rem(a + line + 2 * way - 1, line)}, device_id_type=MESH_ID,
        )

    def goes(way, hop):
        return (a - hop >= 0) & (a + 1 < line) if way else (a + hop < line) & (a >= 1)

    def come(way, hop):
        return a - hop >= 0 if way else a + hop < line

    def pass_along(hop, part):
        for way in (0, 1):
            block = a - hop if way else a + hop
            if hop:

                @pl.when(come(way, hop))
                def _():
                    along(way, block, part).wait_recv()

            @pl.when(goes(way, hop))
            def _():
                along(way, block, part).start()

    def around(turn, kind, part):
        block = (b, b, beside[0], beside[1])[turn]
        first, count = ((0, rows), (0, rows), (0, half), (half, half))[turn]
        spot = row_ref.at[block, pl.ds(kind * rows + first, count), lanes(*parts[part])]
        return pltpu.make_async_remote_copy(
            src_ref=spot, dst_ref=spot, send_sem=wsend.at[turn, kind, part], recv_sem=wrecv.at[turn, kind, part],
            device_id={"state_1": beside[1 - turn % 2]}, device_id_type=MESH_ID,
        )

    def arrive(turn, kind, part):
        block = (beside[0], beside[1], opposite, opposite)[turn]
        first, count = ((0, rows), (0, rows), (0, half), (half, half))[turn]
        spot = row_ref.at[block, pl.ds(kind * rows + first, count), lanes(*parts[part])]
        pltpu.make_async_remote_copy(
            src_ref=spot, dst_ref=spot, send_sem=wsend.at[turn, kind, part], recv_sem=wrecv.at[turn, kind, part],
            device_id={"state_1": beside[1 - turn % 2]}, device_id_type=MESH_ID,
        ).wait_recv()

    def send_around(kind, part):
        for turn in (0, 1):
            around(turn, kind, part).start()

    def pass_around(kind, part):
        for turn in (0, 1):
            arrive(turn, kind, part)
            around(turn + 2, kind, part).start()

    def share(part):
        first, count = parts[part]
        done = v_ref[DEGREE, :, lanes(rim + first, count)]
        col_ref[a, :, lanes(first, count)] = done
        row_ref[b, 0:rows, lanes(first, count)] = done
        pass_along(0, part)
        send_around(0, part)

    for k in range(DEGREE + 1):
        acc_ref[...] = product(picked(k, inner))
        nearby(k).wait_recv()
        if k:
            level(k, part_ref[1] + rcv_ref[k - 1, 1].astype(F32), everyone, zones[1])
        if k == DEGREE:
            share(near)
        acc_ref[...] += product(picked(k, zones[1]))
        base_ref[...] = placed(acc_ref[...].astype(BF16), zones[0])
        for g, group in enumerate(groups):
            afar(k, g).wait_recv()
            if k:
                level(k, part_ref[0, group, :] + rcv_ref[k - 1, 0, group, :].astype(F32), group, zones[0])
            held = v_ref[k, group, zones[0]]
            mine = base_ref[group, :] + own_term(k, group, zones[0])
            for n in (1, 2):
                mine += jnp.dot(held, near_ref[n, :, 0:zone], preferred_element_type=F32)
            part_ref[0, group, :] = mine
            if k < DEGREE:
                snd_ref[k, 0, group, :] = mine.astype(BF16)
            else:
                esnd_ref[0, group, :] = part_ref[0, group, outer[0]].astype(BF16)
            afar(k + 1, g).start()
        if k == DEGREE:
            share(far)
        products = (acc_ref[...] + product(picked(k, zones[0]))).astype(BF16)
        mine = placed(products, zones[1]) + own_term(k, everyone, zones[1])
        part_ref[1] = mine
        if k < DEGREE:
            snd_ref[k, 1] = mine.astype(BF16)
        else:
            esnd_ref[1] = part_ref[1, :, outer[1]].astype(BF16)
        nearby(k + 1).start()
        mine = placed(products, inner) + own_term(k, everyone, inner)
        if k < DEGREE:
            level(k + 1, mine, everyone, inner)
        else:
            filt_ref[...] = v_ref[k, :, rim : rim + nodes]
            row_ref[b, rows : 2 * rows, rim : nodes - rim] = mine.astype(BF16)
            for part in early:
                send_around(1, part)
        if k == DEGREE - 1:
            for part in early:
                share(part)

    def energy(side):
        row_ref[b, rows : 2 * rows, lanes(edges[side], rim)] = (
            part_ref[side, :, own[side]] + ercv_ref[side].astype(F32)
        ).astype(BF16)

    nearby(DEGREE + 1).wait_recv()
    energy(1)
    send_around(1, near)
    for part in early:
        pass_along(1, part)
        pass_around(0, part)
    for g in range(GROUPS):
        afar(DEGREE + 1, g).wait_recv()
    energy(0)
    send_around(1, far)
    for part in (near, far):
        pass_along(1, part)
        pass_around(0, part)
    for hop in range(2, max(line, 3)):
        for part in range(len(parts)):
            pass_along(hop, part)
            if hop == 2:
                pass_around(1, part)
    for kind in (0, 1):
        for part in range(len(parts)):
            for turn in (2, 3):
                arrive(turn, kind, part)

    broad = prcv_ref.shape[2]

    def to_sibling(i):
        return pltpu.make_async_remote_copy(
            src_ref=csnd_ref.at[i], dst_ref=crcv_ref.at[i], send_sem=csend.at[i], recv_sem=crecv.at[i],
            device_id={"space": sibling}, device_id_type=MESH_ID,
        )

    nearest = chip // wide
    order = [lax.rem(nearest + n, line) for n in range(line)]
    about = [lax.rem(b + n, wide) for n in range(wide)]

    for i in order:
        for j in range(wide):
            block = lax.dot_general(col_ref[i], row_ref[j], TRANSPOSED, preferred_element_type=F32)
            for q in (0, 1):
                top, deep = q * half, half // 2
                sum_ref[i, j, q, 0:half, :] = block[top : top + half, 0:broad]
                sum_ref[i, j, q, half : half + deep, :] = jnp.concatenate(
                    [block[top : top + deep, broad:], block[top + deep : top + half, broad:]], axis=1
                )
            csnd_ref[i, j] = sum_ref[i, j, 1 - core].astype(BF16)
        to_sibling(i).start()

    def to_owner(i, j):
        return pltpu.make_async_remote_copy(
            src_ref=psnd_ref.at[i, j], dst_ref=prcv_ref.at[chip], send_sem=psend.at[i, j], recv_sem=precv.at[chip],
            device_id={"state_1": j, "space": 2 * (i * wide + b) + core}, device_id_type=MESH_ID,
        )

    def stays(i, j):
        return (b == j) & (chip == i * wide + b)

    for i in order:
        to_sibling(i).wait_recv()
        for j in about:
            psnd_ref[i, j] = (sum_ref[i, j, core] + crcv_ref[i, j].astype(F32)).astype(BF16)

            @pl.when(stays(i, j))
            def _():
                prcv_ref[chip] = psnd_ref[i, j]

            @pl.when(jnp.logical_not(stays(i, j)))
            def _():
                to_owner(i, j).start()

    total = jnp.zeros(prcv_ref.shape[1:], F32)
    for p in range(chips):

        @pl.when(jnp.logical_not(keeps & (chip == p)))
        def _():
            pltpu.make_async_remote_copy(
                src_ref=prcv_ref.at[p], dst_ref=prcv_ref.at[p], send_sem=precv.at[p], recv_sem=precv.at[p],
                device_id={"space": sibling}, device_id_type=MESH_ID,
            ).wait_recv()

        total += prcv_ref[p].astype(F32)
    total *= 1.0 / (nodes * ring)
    tail = total[half:]
    tail = jnp.concatenate([tail[:, 0 : broad // 2], tail[:, broad // 2 :]], axis=0)
    inter_ref[...] = total[0:half, 0:rows]
    proj_ref[...] = jnp.concatenate([total[0:half, rows:], tail], axis=1)

    for step in range(DEGREE + 2):
        nearby(step).wait_send()
        for g in range(GROUPS):
            afar(step, g).wait_send()
    for way in (0, 1):
        for hop in range(line - 1):
            for part in range(len(parts)):

                @pl.when(goes(way, hop))
                def _():
                    along(way, a - hop if way else a + hop, part).wait_send()

    for turn in range(4):
        for kind in (0, 1):
            for part in range(len(parts)):
                around(turn, kind, part).wait_send()
    for i in range(line):
        to_sibling(i).wait_send()
        for j in range(wide):

            @pl.when(jnp.logical_not(stays(i, j)))
            def _():
                to_owner(i, j).wait_send()


def per_device(states, cell_matrices, connectivity, potential):
    rows, nodes = states.shape
    cells, local, _ = cell_matrices.shape
    line, wide, ring = (lax.axis_size(name) for name in (*STATE, "space"))
    chips, half = ring // 2, rows // 2
    packed = (half + half // 2, 4 * rows // 3)
    rim = local // 4
    ext = nodes + 2 * rim
    vmem = pl.BlockSpec(memory_space=pltpu.VMEM)
    dma = pltpu.SemaphoreType.DMA
    filtered, inter, proj = pl.pallas_call(
        kernel,
        out_shape=(
            jax.ShapeDtypeStruct((rows, nodes), BF16),
            jax.ShapeDtypeStruct((half, rows), F32),
            jax.ShapeDtypeStruct((half, rows), F32),
        ),
        in_specs=[vmem] * 4,
        out_specs=(vmem, vmem, vmem),
        scratch_shapes=[
            pltpu.VMEM((ext, cells * local), BF16),
            pltpu.VMEM((cells * local, ext), BF16),
            pltpu.VMEM((DEGREE + 1, rows, ext), BF16),
            pltpu.VMEM((rows, cells * local), F32),
            pltpu.VMEM((1, ext), F32),
            pltpu.VMEM((3, 2 * rim, cells * local), BF16),
            pltpu.VMEM((rows, 2 * rim), F32),
            pltpu.VMEM((2, rows, 2 * rim), F32),
            pltpu.VMEM((DEGREE, 2, rows, 2 * rim), BF16),
            pltpu.VMEM((DEGREE, 2, rows, 2 * rim), BF16),
            pltpu.VMEM((2, rows, rim), BF16),
            pltpu.VMEM((2, rows, rim), BF16),
            pltpu.VMEM((wide, 2 * rows, nodes), BF16),
            pltpu.VMEM((line, rows, nodes), BF16),
            pltpu.VMEM((line, wide, 2, *packed), F32),
            pltpu.VMEM((line, wide, *packed), BF16),
            pltpu.VMEM((line, wide, *packed), BF16),
            pltpu.VMEM((line, wide, *packed), BF16),
            pltpu.VMEM((chips, *packed), BF16),
            dma((DEGREE + 2, GROUPS)), dma((DEGREE + 2, GROUPS)),
            dma((DEGREE + 2,)), dma((DEGREE + 2,)),
            dma((2, line, PIECES + 2)), dma((line, PIECES + 2)),
            dma((4, 2, PIECES + 2)), dma((4, 2, PIECES + 2)),
            dma((line,)), dma((line,)),
            dma((line, wide)), dma((chips,)),
        ],
        compiler_params=pltpu.CompilerParams(collective_id=0, has_side_effects=True),
    )(states, cell_matrices, connectivity, potential.reshape(1, -1))
    return filtered, inter.T, proj.T


def solution(mesh):
    line = mesh.shape["state"] // WIDE
    finer = Mesh(mesh.devices.reshape(line, WIDE, mesh.shape["space"]), (*STATE, "space"))
    placed = (P(STATE, "space"), P("space", None, None), P("space", None), P("space"))
    return jax.shard_map(
        per_device,
        mesh=finer,
        in_specs=placed,
        out_specs=(P(STATE, "space"), P(STATE, "space"), P(STATE, "space")),
        check_vma=False,
    )
```
